512 devices in a mesh: lon: 64 (over y_hi, z, core), lat: 8 (over x, y_lo).
Axes of the slice: x: 4, y: 8 (y_hi: 4, y_lo: 2; y = y_hi * 2 + y_lo), z: 8, core: 2. Of those that a mesh axis runs over, the one named last changes fastest.
Arguments:
- fine_members: bfloat16 [32, 256, 1024], P(None, 'lon', 'lat'), may hold values from -6 to 6
- coarse_members: bfloat16 [128, 128, 1024], P(None, 'lon', 'lat'), may hold values from -6 to 6
- increments: bfloat16 [32, 256, 1024], P(None, 'lon', 'lat'), may hold values from -0.59765625 to 0.59765625
- level_weights: float32 [2], replicated, may hold values from 0.5 to 2
Outputs:
- applied: float32 [32, 256, 1024], P(None, 'lon', 'lat')
The draws below stay inside these ranges and needn't reach their ends.
All inputs are finite; a program needn't handle non-finite values.
Results may differ from the reference program's by a relative error of at most 0.0055.
Values may be sent and summed in bfloat16 or wider, within the bound.
No kernel may reach another device: no remote copies, remote signals or barrier semaphores. Data moves between devices by JAX's collectives and lax.ppermute only.
A program may use at most 64 MiB of HBM per device.

```python
import math
import jax
import jax.numpy as jnp
from jax import lax

CLON = 4
CLAT = 128
KF = 32
KC = 128
NV = 32
NLON = 256
NLAT = 1024
N_LON = 64
N_LAT = 8


def steps_of(stream_key, shape, pieces, smallest, high):
    gain, own = 1.0, jax.random.fold_in(stream_key, 6)
    for dim, parts in pieces:
        draws = jnp.exp(jax.random.uniform(jax.random.fold_in(own, dim), (parts,), jnp.float32, smallest / len(pieces), high / len(pieces)))
        gain = gain * jnp.repeat(draws, shape[dim] // parts).reshape([-1 if axis == dim else 1 for axis in range(len(shape))])
    return gain


def bell_draw(own_key, shape, deviation, limit, split=(), kind=jnp.bfloat16):
    array = deviation * jax.random.normal(own_key, shape, jnp.float32)
    if split:
        array = array * steps_of(own_key, shape, split, -0.22, 0.18)
    return jnp.clip(array, -limit, limit).astype(kind)


def setup_inputs(seed: int = 0) -> dict:
    keys = jax.random.split(jax.random.key(seed), 5)
    return {
        "fine_members": bell_draw(keys[0], (KF, NLON, NLAT), 1.0, 6.0, ((1, 64), (2, 8))),
        "coarse_members": bell_draw(keys[1], (KC, NLON // 2, NLAT), 1.0, 6.0, ((1, 64), (2, 8))),
        "increments": bell_draw(keys[2], (NV, NLON, NLAT), 0.1, 0.59765625, ((1, 64), (2, 8))),
        "level_weights": jnp.clip(jnp.exp(jax.random.uniform(keys[3], (2,), jnp.float32, math.log(0.5), math.log(2.0))), 0.5, 2.0),
    }


def refine(coarse):
    left_cols = coarse[:, :-1, :]
    right_cols = coarse[:, 1:, :]
    middle = 0.5 * (left_cols + right_cols)
    stacked = jnp.stack((left_cols, middle), axis=2)
    return stacked.reshape(left_cols.shape[0], 2 * left_cols.shape[1], left_cols.shape[2])


def anomalies(members):
    return (members - jnp.mean(members, axis=0, keepdims=True)).astype(jnp.bfloat16)


def profile(distance, extent):
    ratio = distance.astype(jnp.float32) / extent
    return jnp.where(jnp.abs(distance) <= extent, 1.0 - 0.75 * ratio * ratio, 0.0).astype(jnp.float32)


def reference(fine_members, coarse_members, increments, level_weights):
    lon_reach = CLON - 1
    lat_reach = CLAT // 8
    ext_width = CLAT + 2 * lat_reach
    extended = jnp.concatenate((coarse_members, coarse_members[:, :1, :]), axis=1).astype(jnp.float32)
    refined = refine(extended)
    fine_anom = anomalies(fine_members.astype(jnp.float32))
    coarse_anom = anomalies(refined)
    paired_anom = anomalies(refined[:KF])
    stacked = jnp.concatenate((fine_anom, coarse_anom, paired_anom, increments), axis=0)
    padded = jnp.pad(stacked, ((0, 0), (0, 0), (lat_reach, lat_reach)))
    padded = jnp.concatenate((padded[:, -CLON:], padded, padded[:, :CLON]), axis=1)
    lon_profile = profile(jnp.arange(3 * CLON, dtype=jnp.int32)[None, :] - CLON - jnp.arange(CLON, dtype=jnp.int32)[:, None], lon_reach)
    lat_profile = profile(jnp.arange(ext_width, dtype=jnp.int32)[None, :] - lat_reach - jnp.arange(CLAT, dtype=jnp.int32)[:, None], lat_reach)
    taper = (lon_profile[:, None, :, None] * lat_profile[None, :, None, :]).reshape(CLON * CLAT, 3 * CLON * ext_width)
    weight_fine = level_weights[0] / (KF - 1)
    weight_coarse = level_weights[1] / (KC - 1)
    weight_paired = level_weights[1] / (KF - 1)
    member_rows = 2 * KF + KC
    total_rows = member_rows + NV

    def one_tile(index):
        lon_tile = index // N_LAT
        lat_tile = index % N_LAT
        zero_start = jnp.int32(0)
        hood = lax.dynamic_slice(padded, (zero_start, (lon_tile * CLON).astype(jnp.int32), (lat_tile * CLAT).astype(jnp.int32)), (total_rows, 3 * CLON, ext_width))
        own = lax.dynamic_slice(stacked, (zero_start, (lon_tile * CLON).astype(jnp.int32), (lat_tile * CLAT).astype(jnp.int32)), (member_rows, CLON, CLAT))
        hood = hood.reshape(total_rows, 3 * CLON * ext_width)
        own = own.reshape(member_rows, CLON * CLAT)
        first = jnp.dot(own[:KF].T, hood[:KF], preferred_element_type=jnp.float32)
        second = jnp.dot(own[KF:KF + KC].T, hood[KF:KF + KC], preferred_element_type=jnp.float32)
        third = jnp.dot(own[KF + KC:].T, hood[KF + KC:member_rows], preferred_element_type=jnp.float32)
        gram_tile = weight_fine * first + weight_coarse * second - weight_paired * third
        tapered = (taper * gram_tile).astype(jnp.bfloat16)
        return jnp.dot(hood[member_rows:], tapered.T, preferred_element_type=jnp.float32)

    results = lax.map(one_tile, jnp.arange(N_LON * N_LAT, dtype=jnp.int32))
    results = results.reshape(N_LON, N_LAT, NV, CLON, CLAT)
    return jnp.transpose(results, (2, 0, 3, 1, 4)).reshape(NV, N_LON * CLON, N_LAT * CLAT)
```

```python
import functools

import jax
import jax.numpy as jnp
from jax import lax
from jax.experimental import pallas as pl
from jax.experimental.pallas import tpu as pltpu
from jax.sharding import PartitionSpec as P

KF, KC, NV = 32, 128, 32
CLON, CLAT = 4, 128
LON_REACH, LAT_REACH = 3, 16
FV = KF + NV
KX = KF + KC + KF
SENT = 3 * FV + 2 * KC
EDGE = KC + 2 * FV
COLUMNS = range(1, 11)
VMEM = pl.BlockSpec(memory_space=pltpu.VMEM)
SMEM = pl.BlockSpec(memory_space=pltpu.SMEM)
F32, BF16 = jnp.float32, jnp.bfloat16

OWN_FV = (0, 64, 128, 448)
OWN_C = (192, 320)
WEST_FV = (None, 0, 64, 384)
WEST_C = (128, 256)
EAST_FV = (0, 64, 128, None)
EAST_C = (192, 320)


def lon_weight(distance):
    return 1.0 - 0.75 * (distance / LON_REACH) ** 2


def fv_block(west, own, east, column):
    tile, at = divmod(column, CLON)
    ref, offsets = ((west, WEST_FV), (own, OWN_FV), (east, EAST_FV))[tile]
    return ref, offsets[at]


def coarse_block(west, own, east, column):
    tile, at = divmod(column, 2)
    ref, offsets = ((west, WEST_C), (own, OWN_C), (east, EAST_C))[tile]
    return ref, offsets[at]


def pack_kernel(fine, coarse, vectors, own, to_west, to_east, fine32, coarse32, vectors32):
    fine32[...] = fine[...].astype(F32)
    coarse32[...] = coarse[...].astype(F32)
    vectors32[...] = vectors[...].astype(F32)

    def put(block, at):
        rows = block.shape[0]
        own[at : at + rows, :] = block
        if at < SENT:
            to_west[at : at + rows, :] = block
        if at >= FV:
            to_east[at - FV : at - FV + rows, :] = block

    for a in range(CLON):
        put(fine32[pl.ds(a, KF, stride=CLON), :].astype(BF16), OWN_FV[a])
        put(vectors32[pl.ds(a, NV, stride=CLON), :].astype(BF16), OWN_FV[a] + KF)
    for m in range(2):
        put(coarse32[pl.ds(m, KC, stride=2), :].astype(BF16), OWN_C[m])


def edge_kernel(west, own, east, up, down):
    lane = lax.broadcasted_iota(jnp.int32, (1, CLAT), 1) // LAT_REACH

    def gather(blocks, rows, at):
        high = jnp.zeros((rows, CLAT), F32)
        low = jnp.zeros((rows, CLAT), F32)
        for slot, (ref, offset) in blocks:
            block = ref[offset : offset + rows, :].astype(F32)
            start = slot * LAT_REACH
            shift = (start - (CLAT - LAT_REACH)) % CLAT
            high = jnp.where(lane == slot, pltpu.roll(block, shift, 1) if shift else block, high)
            low = jnp.where(lane == slot, pltpu.roll(block, start, 1) if start else block, low)
        up[at : at + rows, :] = high.astype(BF16)
        down[at : at + rows, :] = low.astype(BF16)

    gather([(m, coarse_block(west, own, east, m)) for m in range(6)], KC, 0)
    gather([(m, fv_block(west, own, east, 2 * m)) for m in range(1, 6)], FV, KC)
    gather([(m, fv_block(west, own, east, 2 * m + 1)) for m in range(0, 5)], FV, KC + FV)


def anomaly_rows(fine, refined):
    fine = fine - jnp.mean(fine, axis=0, keepdims=True)
    coarse = refined - jnp.mean(refined, axis=0, keepdims=True)
    paired = refined[:KF]
    paired = paired - jnp.mean(paired, axis=0, keepdims=True)
    return fine, coarse, paired


def core_kernel(weights, west, own, east, out, edges, hood, mine, vectors, taper):
    i = lax.broadcasted_iota(jnp.int32, (CLAT, CLAT), 0)
    j = lax.broadcasted_iota(jnp.int32, (CLAT, CLAT), 1)
    gap = jnp.abs(i - j)
    ratio = gap.astype(F32) * (1.0 / LAT_REACH)
    band = jnp.where(gap <= LAT_REACH, 1.0 - 0.75 * ratio * ratio, 0.0)
    for distance in range(LON_REACH + 1):
        taper[distance] = band * lon_weight(distance)
    weight_fine = weights[0] * (1.0 / (KF - 1))
    weight_coarse = weights[1] * (1.0 / (KC - 1))
    weight_paired = weights[1] * (-1.0 / (KF - 1))
    lane = lax.broadcasted_iota(jnp.int32, (1, CLAT), 1) // LAT_REACH
    top = jnp.zeros((KX, CLAT), F32)
    bottom = jnp.zeros((KX, CLAT), F32)
    for b in COLUMNS:
        ref, at = fv_block(west, own, east, b)
        ref_c, at_c = coarse_block(west, own, east, b // 2)
        refined = ref_c[at_c : at_c + KC, :].astype(F32)
        if b % 2:
            ref_n, at_n = coarse_block(west, own, east, b // 2 + 1)
            refined = 0.5 * (refined + ref_n[at_n : at_n + KC, :].astype(F32))
        fine, coarse, paired = anomaly_rows(ref[at : at + KF, :].astype(F32), refined)
        lanes = slice((b - 1) * CLAT, b * CLAT)
        hood[:KF, lanes] = fine.astype(BF16)
        hood[KF : KF + KC, lanes] = coarse.astype(BF16)
        hood[KF + KC :, lanes] = paired.astype(BF16)
        vectors[:, lanes] = ref[at + KF : at + FV, :]
        if CLON <= b < 2 * CLON:
            a = b - CLON
            scaled = jnp.concatenate(
                (weight_fine * fine, weight_coarse * coarse, weight_paired * paired), axis=0
            )
            mine[:, a * CLAT : (a + 1) * CLAT] = scaled.astype(BF16)
            shift = ((a - 7) * LAT_REACH) % CLAT
            top = jnp.where(lane == a, pltpu.roll(scaled, shift, 1), top)
            bottom = jnp.where(
                lane == a, pltpu.roll(scaled, a * LAT_REACH, 1) if a else scaled, bottom
            )
    edges[0] = top.astype(BF16)
    edges[1] = bottom.astype(BF16)
    for a in range(CLON):
        lanes = slice(a * CLAT, (a + 7) * CLAT)
        gram = lax.dot_general(
            mine[:, a * CLAT : (a + 1) * CLAT],
            hood[:, lanes],
            (((0,), (0,)), ((), ())),
            preferred_element_type=F32,
        )
        tapered = jnp.concatenate(
            [
                (taper[abs(n - LON_REACH)] * gram[:, n * CLAT : (n + 1) * CLAT]).astype(BF16)
                for n in range(7)
            ],
            axis=1,
        )
        out[a] = lax.dot_general(
            vectors[:, lanes], tapered, (((1,), (1,)), ((), ())), preferred_element_type=F32
        )


def rim_taper(parity, side):
    row = lax.broadcasted_iota(jnp.int32, (CLON * LAT_REACH, CLAT), 0)
    lane = lax.broadcasted_iota(jnp.int32, (CLON * LAT_REACH, CLAT), 1)
    lon_gap = jnp.abs(2 * (lane // LAT_REACH) + parity - CLON - row // LAT_REACH)
    shift = lane % LAT_REACH - row % LAT_REACH
    lat_gap = LAT_REACH + shift if side == 0 else LAT_REACH - shift
    lon_ratio = lon_gap.astype(F32) * (1.0 / LON_REACH)
    lat_ratio = lat_gap.astype(F32) * (1.0 / LAT_REACH)
    inside = jnp.logical_and(lon_gap <= LON_REACH, lat_gap <= LAT_REACH)
    value = (1.0 - 0.75 * lon_ratio * lon_ratio) * (1.0 - 0.75 * lat_ratio * lat_ratio)
    return jnp.where(inside, value, 0.0)


def rim_kernel(core, edges, above, below, out, result32):
    lane = lax.broadcasted_iota(jnp.int32, (1, CLAT), 1) // LAT_REACH
    totals = [core[a] for a in range(CLON)]
    for side, rim in ((0, above), (1, below)):
        plain = rim[:KC, :].astype(F32)
        halfway = 0.5 * (plain + pltpu.roll(plain, CLAT - LAT_REACH, 1))
        mine = edges[side]
        added = None
        for parity, refined in ((0, plain), (1, halfway)):
            at = KC + parity * FV
            rows = anomaly_rows(rim[at : at + KF, :].astype(F32), refined)
            hood = jnp.concatenate([part.astype(BF16) for part in rows], axis=0)
            gram = lax.dot_general(
                mine, hood, (((0,), (0,)), ((), ())), preferred_element_type=F32
            )[: CLON * LAT_REACH]
            tapered = (rim_taper(parity, side) * gram).astype(BF16)
            tapered = jnp.concatenate((tapered, jnp.zeros_like(tapered)), axis=0)
            term = lax.dot_general(
                rim[at + KF : at + FV, :],
                tapered,
                (((1,), (1,)), ((), ())),
                preferred_element_type=F32,
            )
            added = term if added is None else added + term
        slot = 7 if side == 0 else 0
        for a in range(CLON):
            shift = ((slot - a) * LAT_REACH) % CLAT
            moved = pltpu.roll(added, shift, 1) if shift else added
            totals[a] = totals[a] + jnp.where(lane == slot, moved, 0.0)
    for a in range(CLON):
        result32[pl.ds(a, NV, stride=CLON), :] = totals[a]
    out[...] = result32[...]


def call(kernel, outs, in_specs, scratch, flops, moved):
    return pl.pallas_call(
        kernel,
        out_shape=[jax.ShapeDtypeStruct(shape, dtype) for shape, dtype in outs],
        in_specs=in_specs,
        out_specs=[VMEM] * len(outs),
        scratch_shapes=[pltpu.VMEM(shape, dtype) for shape, dtype in scratch],
        compiler_params=pltpu.CompilerParams(vmem_limit_bytes=24 << 20),
        cost_estimate=pl.CostEstimate(flops=flops, bytes_accessed=moved, transcendentals=0),
    )


def shift_lon(block, by):
    n = lax.axis_size("lon")
    return lax.ppermute(block, "lon", [(k, (k + by) % n) for k in range(n)])


def shift_lat(block, by):
    n = lax.axis_size("lat")
    return lax.ppermute(block, "lat", [(k, k + by) for k in range(n) if 0 <= k + by < n])


def per_device(fine_members, coarse_members, increments, level_weights):
    own, to_west, to_east = call(
        pack_kernel,
        [((512, CLAT), BF16), ((SENT, CLAT), BF16), ((SENT, CLAT), BF16)],
        [VMEM] * 3,
        [((128, CLAT), F32), ((256, CLAT), F32), ((128, CLAT), F32)],
        1 << 20,
        1 << 19,
    )(
        fine_members.reshape(KF * CLON, CLAT),
        coarse_members.reshape(KC * 2, CLAT),
        increments.reshape(NV * CLON, CLAT),
    )
    west = shift_lon(to_east, 1)
    east = shift_lon(to_west, -1)
    up, down = call(
        edge_kernel,
        [((EDGE, CLAT), BF16), ((EDGE, CLAT), BF16)],
        [VMEM] * 3,
        [],
        1 << 20,
        1 << 19,
    )(west, own, east)
    below = shift_lat(up, 1)
    above = shift_lat(down, -1)
    core, edges = call(
        core_kernel,
        [((CLON, NV, CLAT), F32), ((2, KX, CLAT), BF16)],
        [SMEM] + [VMEM] * 3,
        [
            ((KX, 10 * CLAT), BF16),
            ((KX, CLON * CLAT), BF16),
            ((NV, 10 * CLAT), BF16),
            ((LON_REACH + 1, CLAT, CLAT), F32),
        ],
        200 << 20,
        4 << 20,
    )(level_weights, west, own, east)
    (out,) = call(
        rim_kernel,
        [((NV * CLON, CLAT), F32)],
        [VMEM] * 4,
        [((NV * CLON, CLAT), F32)],
        8 << 20,
        1 << 19,
    )(core, edges, above, below)
    return out.reshape(NV, CLON, CLAT)


def solution(mesh):
    in_specs = (P(None, "lon", "lat"), P(None, "lon", "lat"), P(None, "lon", "lat"), P())
    out_specs = P(None, "lon", "lat")
    return jax.shard_map(
        per_device, mesh=mesh, in_specs=in_specs, out_specs=out_specs, check_vma=False
    )
```

```python
import jax
import jax.numpy as jnp
from jax import lax
from jax.experimental import pallas as pl
from jax.experimental.pallas import tpu as pltpu
from jax.sharding import PartitionSpec as P

KF, KC, NV = 32, 128, 32
CLON, CLAT = 4, 128
LON_REACH, LAT_REACH = 3, 16
FV = KF + NV
KX = KF + KC + KF
SENT = 3 * FV + 2 * KC
EDGE = KC + 2 * FV
COLUMNS = range(1, 11)
VMEM = pl.BlockSpec(memory_space=pltpu.VMEM)
SMEM = pl.BlockSpec(memory_space=pltpu.SMEM)
F32, BF16 = jnp.float32, jnp.bfloat16

OWN_FV = (0, 64, 128, 448)
OWN_C = (192, 320)
WEST_FV = (None, 0, 64, 384)
WEST_C = (128, 256)
EAST_FV = (0, 64, 128, None)
EAST_C = (192, 320)


def lon_weight(distance):
    return 1.0 - 0.75 * (distance / LON_REACH) ** 2


def fv_block(west, own, east, column):
    tile, at = divmod(column, CLON)
    ref, offsets = ((west, WEST_FV), (own, OWN_FV), (east, EAST_FV))[tile]
    return ref, offsets[at]


def coarse_block(west, own, east, column):
    tile, at = divmod(column, 2)
    ref, offsets = ((west, WEST_C), (own, OWN_C), (east, EAST_C))[tile]
    return ref, offsets[at]


def pack_kernel(
    fine, coarse, vectors, own, off_chip, on_chip, fine16, coarse16, vectors16, fine32, coarse32, vectors32, sem
):
    pairs = ((fine, fine16), (coarse, coarse16), (vectors, vectors16))
    copies = [pltpu.make_async_copy(src, dst, sem.at[n]) for n, (src, dst) in enumerate(pairs)]
    for copy in copies:
        copy.start()
    odd = lax.axis_index("lon") % 2 == 1

    def put(block, at):
        own[at : at + block.shape[0], :] = block

    copies[0].wait()
    fine32[...] = fine16[...].astype(F32)
    for a in range(CLON):
        put(fine32[pl.ds(a, KF, stride=CLON), :].astype(BF16), OWN_FV[a])
    copies[1].wait()
    coarse32[...] = coarse16[...].astype(F32)
    for m in range(2):
        put(coarse32[pl.ds(m, KC, stride=2), :].astype(BF16), OWN_C[m])
    copies[2].wait()
    vectors32[...] = vectors16[...].astype(F32)
    for a in range(CLON):
        put(vectors32[pl.ds(a, NV, stride=CLON), :].astype(BF16), OWN_FV[a] + KF)
    to_west, to_east = own[:SENT, :], own[FV:, :]
    off_chip[...] = jnp.where(odd, to_east, to_west)
    on_chip[...] = jnp.where(odd, to_west, to_east)


def sort_sides(off_chip, on_chip, west, east):
    odd = lax.axis_index("lon") % 2 == 1
    off, on = off_chip[...], on_chip[...]
    west[...] = jnp.where(odd, on, off)
    east[...] = jnp.where(odd, off, on)


def edge_kernel(off_chip, own, on_chip, up, down, west, east):
    sort_sides(off_chip, on_chip, west, east)
    lane = lax.broadcasted_iota(jnp.int32, (1, CLAT), 1) // LAT_REACH

    def gather(blocks, rows, at):
        high = jnp.zeros((rows, CLAT), F32)
        low = jnp.zeros((rows, CLAT), F32)
        for slot, (ref, offset) in blocks:
            block = ref[offset : offset + rows, :].astype(F32)
            start = slot * LAT_REACH
            shift = (start - (CLAT - LAT_REACH)) % CLAT
            high = jnp.where(lane == slot, pltpu.roll(block, shift, 1) if shift else block, high)
            low = jnp.where(lane == slot, pltpu.roll(block, start, 1) if start else block, low)
        up[at : at + rows, :] = high.astype(BF16)
        down[at : at + rows, :] = low.astype(BF16)

    gather([(m, coarse_block(west, own, east, m)) for m in range(6)], KC, 0)
    gather([(m, fv_block(west, own, east, 2 * m)) for m in range(1, 6)], FV, KC)
    gather([(m, fv_block(west, own, east, 2 * m + 1)) for m in range(0, 5)], FV, KC + FV)


def anomaly_rows(fine, refined):
    fine = fine - jnp.mean(fine, axis=0, keepdims=True)
    coarse = refined - jnp.mean(refined, axis=0, keepdims=True)
    paired = refined[:KF]
    paired = paired - jnp.mean(paired, axis=0, keepdims=True)
    return fine, coarse, paired


def rim_taper(parity, side):
    row = lax.broadcasted_iota(jnp.int32, (CLON * LAT_REACH, CLAT), 0)
    lane = lax.broadcasted_iota(jnp.int32, (CLON * LAT_REACH, CLAT), 1)
    lon_gap = jnp.abs(2 * (lane // LAT_REACH) + parity - CLON - row // LAT_REACH)
    shift = lane % LAT_REACH - row % LAT_REACH
    lat_gap = LAT_REACH + shift if side == 0 else LAT_REACH - shift
    lon_ratio = lon_gap.astype(F32) * (1.0 / LON_REACH)
    lat_ratio = lat_gap.astype(F32) * (1.0 / LAT_REACH)
    inside = jnp.logical_and(lon_gap <= LON_REACH, lat_gap <= LAT_REACH)
    value = (1.0 - 0.75 * lon_ratio * lon_ratio) * (1.0 - 0.75 * lat_ratio * lat_ratio)
    return jnp.where(inside, value, 0.0)


def core_kernel(
    weights, off_chip, own, on_chip, out, edges, rims, hood, mine, vectors, taper, west, east
):
    sort_sides(off_chip, on_chip, west, east)
    i = lax.broadcasted_iota(jnp.int32, (CLAT, CLAT), 0)
    j = lax.broadcasted_iota(jnp.int32, (CLAT, CLAT), 1)
    gap = jnp.abs(i - j)
    ratio = gap.astype(F32) * (1.0 / LAT_REACH)
    band = jnp.where(gap <= LAT_REACH, 1.0 - 0.75 * ratio * ratio, 0.0)
    for distance in range(LON_REACH + 1):
        taper[distance] = band * lon_weight(distance)
    weight_fine = weights[0] * (1.0 / (KF - 1))
    weight_coarse = weights[1] * (1.0 / (KC - 1))
    weight_paired = weights[1] * (-1.0 / (KF - 1))
    lane = lax.broadcasted_iota(jnp.int32, (1, CLAT), 1) // LAT_REACH
    top = jnp.zeros((KX, CLAT), F32)
    bottom = jnp.zeros((KX, CLAT), F32)
    for b in COLUMNS:
        ref, at = fv_block(west, own, east, b)
        ref_c, at_c = coarse_block(west, own, east, b // 2)
        refined = ref_c[at_c : at_c + KC, :].astype(F32)
        if b % 2:
            ref_n, at_n = coarse_block(west, own, east, b // 2 + 1)
            refined = 0.5 * (refined + ref_n[at_n : at_n + KC, :].astype(F32))
        fine, coarse, paired = anomaly_rows(ref[at : at + KF, :].astype(F32), refined)
        lanes = slice((b - 1) * CLAT, b * CLAT)
        hood[:KF, lanes] = fine.astype(BF16)
        hood[KF : KF + KC, lanes] = coarse.astype(BF16)
        hood[KF + KC :, lanes] = paired.astype(BF16)
        vectors[:, lanes] = ref[at + KF : at + FV, :]
        if CLON <= b < 2 * CLON:
            a = b - CLON
            scaled = jnp.concatenate(
                (weight_fine * fine, weight_coarse * coarse, weight_paired * paired), axis=0
            )
            mine[:, a * CLAT : (a + 1) * CLAT] = scaled.astype(BF16)
            shift = ((a - 7) * LAT_REACH) % CLAT
            top = jnp.where(lane == a, pltpu.roll(scaled, shift, 1), top)
            bottom = jnp.where(
                lane == a, pltpu.roll(scaled, a * LAT_REACH, 1) if a else scaled, bottom
            )
    for side, rim in ((0, top), (1, bottom)):
        edges[side] = rim.T[: CLON * LAT_REACH].astype(BF16)
        for parity in range(2):
            rims[side, :, parity * CLAT : (parity + 1) * CLAT] = rim_taper(parity, side)
    for a in range(CLON):
        lanes = slice(a * CLAT, (a + 7) * CLAT)
        gram = lax.dot_general(
            mine[:, a * CLAT : (a + 1) * CLAT],
            hood[:, lanes],
            (((0,), (0,)), ((), ())),
            preferred_element_type=F32,
        )
        tapered = jnp.concatenate(
            [
                (taper[abs(n - LON_REACH)] * gram[:, n * CLAT : (n + 1) * CLAT]).astype(BF16)
                for n in range(7)
            ],
            axis=1,
        )
        out[a] = lax.dot_general(
            vectors[:, lanes], tapered, (((1,), (1,)), ((), ())), preferred_element_type=F32
        )


def rim_kernel(core, edges, rims, above, below, out, result32, hood):
    lane = lax.broadcasted_iota(jnp.int32, (1, CLAT), 1) // LAT_REACH
    totals = [core[a] for a in range(CLON)]
    for side, rim in ((0, above), (1, below)):
        plain = rim[:KC, :].astype(F32)
        halfway = 0.5 * (plain + pltpu.roll(plain, CLAT - LAT_REACH, 1))
        vectors = []
        for parity, refined in ((0, plain), (1, halfway)):
            at = KC + parity * FV
            fine, coarse, paired = anomaly_rows(rim[at : at + KF, :].astype(F32), refined)
            lanes = slice(parity * CLAT, (parity + 1) * CLAT)
            hood[side, :KF, lanes] = fine.astype(BF16)
            hood[side, KF : KF + KC, lanes] = coarse.astype(BF16)
            hood[side, KF + KC :, lanes] = paired.astype(BF16)
            vectors.append(rim[at + KF : at + FV, :])
        gram = jnp.dot(edges[side], hood[side], preferred_element_type=F32)
        tapered = (rims[side] * gram).astype(BF16)
        tapered = jnp.concatenate((tapered, jnp.zeros_like(tapered)), axis=0)
        added = lax.dot_general(
            jnp.concatenate(vectors, axis=1),
            tapered,
            (((1,), (1,)), ((), ())),
            preferred_element_type=F32,
        )
        slot = 7 if side == 0 else 0
        for a in range(CLON):
            shift = ((slot - a) * LAT_REACH) % CLAT
            moved = pltpu.roll(added, shift, 1) if shift else added
            totals[a] = totals[a] + jnp.where(lane == slot, moved, 0.0)
    for a in range(CLON):
        result32[pl.ds(a, NV, stride=CLON), :] = totals[a]
    out[...] = result32[...]


def call(kernel, outs, in_specs, scratch, flops, moved):
    return pl.pallas_call(
        kernel,
        out_shape=[jax.ShapeDtypeStruct(shape, dtype) for shape, dtype in outs],
        in_specs=in_specs,
        out_specs=[VMEM] * len(outs),
        scratch_shapes=scratch,
        compiler_params=pltpu.CompilerParams(vmem_limit_bytes=24 << 20),
        cost_estimate=pl.CostEstimate(flops=flops, bytes_accessed=moved, transcendentals=0),
    )


def in_hbm(array):
    return pltpu.with_memory_space_constraint(array, pltpu.HBM)


def swap(block, axis, first, wraps):
    n = lax.axis_size(axis)
    pairs = [(k, ((k - first) ^ 1) + first) for k in range(n)]
    pairs = [(k, to % n) for k, to in pairs if wraps or 0 <= to < n]
    return lax.ppermute(block, axis, pairs)


def shift_lat(block, by):
    n = lax.axis_size("lat")
    return lax.ppermute(block, "lat", [(k, k + by) for k in range(n) if 0 <= k + by < n])


def per_device(fine_members, coarse_members, increments, level_weights):
    shapes = ((128, CLAT), (256, CLAT), (128, CLAT))
    received = [pltpu.VMEM((SENT, CLAT), BF16)] * 2
    own, off_chip, on_chip = call(
        pack_kernel,
        [((512, CLAT), BF16), ((SENT, CLAT), BF16), ((SENT, CLAT), BF16)],
        [pl.BlockSpec(memory_space=pltpu.HBM)] * 3,
        [pltpu.VMEM(shape, BF16) for shape in shapes]
        + [pltpu.VMEM(shape, F32) for shape in shapes]
        + [pltpu.SemaphoreType.DMA((3,))],
        1 << 20,
        1 << 19,
    )(
        in_hbm(fine_members.reshape(KF * CLON, CLAT)),
        in_hbm(coarse_members.reshape(KC * 2, CLAT)),
        in_hbm(increments.reshape(NV * CLON, CLAT)),
    )
    off_chip = swap(off_chip, "lon", 1, True)
    on_chip = swap(on_chip, "lon", 0, True)
    up, down = call(
        edge_kernel,
        [((EDGE, CLAT), BF16), ((EDGE, CLAT), BF16)],
        [VMEM] * 3,
        received,
        1 << 20,
        1 << 19,
    )(off_chip, own, on_chip)
    below = shift_lat(up, 1)
    above = shift_lat(down, -1)
    core, edges, rims = call(
        core_kernel,
        [
            ((CLON, NV, CLAT), F32),
            ((2, CLON * LAT_REACH, KX), BF16),
            ((2, CLON * LAT_REACH, 2 * CLAT), F32),
        ],
        [SMEM] + [VMEM] * 3,
        [
            pltpu.VMEM((KX, 10 * CLAT), BF16),
            pltpu.VMEM((KX, CLON * CLAT), BF16),
            pltpu.VMEM((NV, 10 * CLAT), BF16),
            pltpu.VMEM((LON_REACH + 1, CLAT, CLAT), F32),
        ]
        + received,
        200 << 20,
        4 << 20,
    )(level_weights, off_chip, own, on_chip)
    (out,) = call(
        rim_kernel,
        [((NV * CLON, CLAT), F32)],
        [VMEM] * 5,
        [pltpu.VMEM((NV * CLON, CLAT), F32), pltpu.VMEM((2, KX, 2 * CLAT), BF16)],
        8 << 20,
        1 << 19,
    )(core, edges, rims, above, below)
    return out.reshape(NV, CLON, CLAT)


def solution(mesh):
    in_specs = (P(None, "lon", "lat"), P(None, "lon", "lat"), P(None, "lon", "lat"), P())
    out_specs = P(None, "lon", "lat")
    return jax.shard_map(
        per_device, mesh=mesh, in_specs=in_specs, out_specs=out_specs, check_vma=False
    )
```

```python
import jax
import jax.numpy as jnp
from jax import lax
from jax.experimental import pallas as pl
from jax.experimental.pallas import tpu as pltpu
from jax.sharding import PartitionSpec as P

KF, KC, NV = 32, 128, 32
CLON, CLAT = 4, 128
LON_REACH, LAT_REACH = 3, 16
FV = KF + NV
KX = KF + KC + KF
SENT = 3 * FV + 2 * KC
EDGE = KC + 2 * FV
COLUMNS = range(1, 11)
VMEM = pl.BlockSpec(memory_space=pltpu.VMEM)
SMEM = pl.BlockSpec(memory_space=pltpu.SMEM)
F32, BF16 = jnp.float32, jnp.bfloat16

OWN_FV = (0, 64, 128, 448)
OWN_C = (192, 320)
WEST_FV = (None, 0, 64, 384)
WEST_C = (128, 256)
EAST_FV = (0, 64, 128, None)
EAST_C = (192, 320)


def lon_weight(distance):
    return 1.0 - 0.75 * (distance / LON_REACH) ** 2


class Hood:
    def __init__(self, off_chip, own, on_chip):
        self.off_chip, self.own, self.on_chip = off_chip, own, on_chip
        self.odd = lax.axis_index("lon") % 2 == 1

    def rows(self, tile, at, count):
        if tile == 1:
            return self.own[at : at + count, :]
        off, on = self.off_chip[at : at + count, :], self.on_chip[at : at + count, :]
        return jnp.where(self.odd, on, off) if tile == 0 else jnp.where(self.odd, off, on)

    def fv(self, column):
        tile, at = divmod(column, CLON)
        return self.rows(tile, (WEST_FV, OWN_FV, EAST_FV)[tile][at], FV)

    def coarse(self, column):
        tile, at = divmod(column, 2)
        return self.rows(tile, (WEST_C, OWN_C, EAST_C)[tile][at], KC)


def pack_kernel(
    fine, coarse, vectors, own, off_chip, on_chip, fine16, coarse16, vectors16, fine32, coarse32, vectors32, sem
):
    pairs = ((fine, fine16), (coarse, coarse16), (vectors, vectors16))
    copies = [pltpu.make_async_copy(src, dst, sem.at[n]) for n, (src, dst) in enumerate(pairs)]
    for copy in copies:
        copy.start()
    odd = lax.axis_index("lon") % 2 == 1

    def put(block, at):
        own[at : at + block.shape[0], :] = block

    copies[0].wait()
    fine32[...] = fine16[...].astype(F32)
    for a in range(CLON):
        put(fine32[pl.ds(a, KF, stride=CLON), :].astype(BF16), OWN_FV[a])
    copies[1].wait()
    coarse32[...] = coarse16[...].astype(F32)
    for m in range(2):
        put(coarse32[pl.ds(m, KC, stride=2), :].astype(BF16), OWN_C[m])
    copies[2].wait()
    vectors32[...] = vectors16[...].astype(F32)
    for a in range(CLON):
        put(vectors32[pl.ds(a, NV, stride=CLON), :].astype(BF16), OWN_FV[a] + KF)
    to_west, to_east = own[:SENT, :], own[FV:, :]
    off_chip[...] = jnp.where(odd, to_east, to_west)
    on_chip[...] = jnp.where(odd, to_west, to_east)


def edge_kernel(off_chip, own, on_chip, near, far):
    hood = Hood(off_chip, own, on_chip)
    odd = lax.axis_index("lat") % 2 == 1
    lane = lax.broadcasted_iota(jnp.int32, (1, CLAT), 1) // LAT_REACH

    def gather(blocks, rows, at):
        high = jnp.zeros((rows, CLAT), F32)
        low = jnp.zeros((rows, CLAT), F32)
        for slot, block in blocks:
            moved = pltpu.roll(block.astype(F32), (slot + 1) * LAT_REACH, 1)
            high = jnp.where(lane == slot, moved, high)
            low = jnp.where(lane == slot + 1, moved, low)
        near[at : at + rows, :] = jnp.where(odd, low, high).astype(BF16)
        far[at : at + rows, :] = jnp.where(odd, high, low).astype(BF16)

    gather([(m, hood.coarse(m)) for m in range(6)], KC, 0)
    gather([(m, hood.fv(2 * m)) for m in range(1, 6)], FV, KC)
    gather([(m, hood.fv(2 * m + 1)) for m in range(0, 5)], FV, KC + FV)


def anomaly_rows(fine, refined):
    fine = fine - jnp.mean(fine, axis=0, keepdims=True)
    coarse = refined - jnp.mean(refined, axis=0, keepdims=True)
    paired = refined[:KF]
    paired = paired - jnp.mean(paired, axis=0, keepdims=True)
    return fine, coarse, paired


def rim_taper(side, parity):
    row = lax.broadcasted_iota(jnp.int32, (CLAT, CLAT), 0)
    lane = lax.broadcasted_iota(jnp.int32, (CLAT, CLAT), 1)
    column = 2 * (lane // LAT_REACH - (1 - side)) + parity
    lon_gap = jnp.abs(column - CLON - row // (2 * LAT_REACH))
    shift = lane % LAT_REACH - row % LAT_REACH
    lat_gap = LAT_REACH + shift if side == 0 else LAT_REACH - shift
    lon_ratio = lon_gap.astype(F32) * (1.0 / LON_REACH)
    lat_ratio = lat_gap.astype(F32) * (1.0 / LAT_REACH)
    here = row // LAT_REACH % 2 == side
    inside = here & (lon_gap <= LON_REACH) & (lat_gap <= LAT_REACH)
    value = (1.0 - 0.75 * lon_ratio * lon_ratio) * (1.0 - 0.75 * lat_ratio * lat_ratio)
    return jnp.where(inside, value, 0.0)


def core_kernel(
    weights, off_chip, own, on_chip, out, edges, rims, hood, mine, vectors, taper
):
    tiles = Hood(off_chip, own, on_chip)
    i = lax.broadcasted_iota(jnp.int32, (CLAT, CLAT), 0)
    j = lax.broadcasted_iota(jnp.int32, (CLAT, CLAT), 1)
    gap = jnp.abs(i - j)
    ratio = gap.astype(F32) * (1.0 / LAT_REACH)
    band = jnp.where(gap <= LAT_REACH, 1.0 - 0.75 * ratio * ratio, 0.0)
    for distance in range(LON_REACH + 1):
        taper[distance] = band * lon_weight(distance)
    weight_fine = weights[0] * (1.0 / (KF - 1))
    weight_coarse = weights[1] * (1.0 / (KC - 1))
    weight_paired = weights[1] * (-1.0 / (KF - 1))
    lane = lax.broadcasted_iota(jnp.int32, (1, CLAT), 1) // LAT_REACH
    both = jnp.zeros((KX, CLAT), F32)
    coarse_columns = [tiles.coarse(m).astype(F32) for m in range(6)]
    for b in COLUMNS:
        block = tiles.fv(b)
        refined = coarse_columns[b // 2]
        if b % 2:
            refined = 0.5 * (refined + coarse_columns[b // 2 + 1])
        fine, coarse, paired = anomaly_rows(block[:KF].astype(F32), refined)
        lanes = slice((b - 1) * CLAT, b * CLAT)
        hood[:KF, lanes] = fine.astype(BF16)
        hood[KF : KF + KC, lanes] = coarse.astype(BF16)
        hood[KF + KC :, lanes] = paired.astype(BF16)
        vectors[:, lanes] = block[KF:]
        if CLON <= b < 2 * CLON:
            a = b - CLON
            scaled = jnp.concatenate(
                (weight_fine * fine, weight_coarse * coarse, weight_paired * paired), axis=0
            )
            mine[:, a * CLAT : (a + 1) * CLAT] = scaled.astype(BF16)
            moved = pltpu.roll(scaled, (2 * a + 1) * LAT_REACH, 1)
            both = jnp.where(lane // 2 == a, moved, both)
    edges[...] = both.T.astype(BF16)
    for side in range(2):
        for parity in range(2):
            at = (2 * side + parity) * CLAT
            rims[:, at : at + CLAT] = rim_taper(side, parity)
    for a in range(CLON):
        lanes = slice(a * CLAT, (a + 7) * CLAT)
        gram = lax.dot_general(
            mine[:, a * CLAT : (a + 1) * CLAT],
            hood[:, lanes],
            (((0,), (0,)), ((), ())),
            preferred_element_type=F32,
        )
        tapered = jnp.concatenate(
            [
                (taper[abs(n - LON_REACH)] * gram[:, n * CLAT : (n + 1) * CLAT]).astype(BF16)
                for n in range(7)
            ],
            axis=1,
        )
        out[a] = lax.dot_general(
            vectors[:, lanes], tapered, (((1,), (1,)), ((), ())), preferred_element_type=F32
        )


def halfway(values):
    return 0.5 * (values + pltpu.roll(values, CLAT - LAT_REACH, 1))


def rim_kernel(core, edges, rims, near, far, out, result32):
    odd = lax.axis_index("lat") % 2 == 1
    near, far = near[...], far[...]
    hood, vectors = [], []
    for rim in (jnp.where(odd, far, near), jnp.where(odd, near, far)):
        refined = rim[:KC].astype(F32)
        coarse = refined - jnp.mean(refined, axis=0, keepdims=True)
        paired = refined[:KF] - jnp.mean(refined[:KF], axis=0, keepdims=True)
        for at, pair in ((KC, (coarse, paired)), (KC + FV, (halfway(coarse), halfway(paired)))):
            fine = rim[at : at + KF].astype(F32)
            fine = fine - jnp.mean(fine, axis=0, keepdims=True)
            hood.append(jnp.concatenate([part.astype(BF16) for part in (fine, *pair)], axis=0))
            vectors.append(rim[at + KF : at + FV])
    gram = jnp.dot(edges[...], jnp.concatenate(hood, axis=1), preferred_element_type=F32)
    added = lax.dot_general(
        jnp.concatenate(vectors, axis=1),
        (rims[...] * gram).astype(BF16),
        (((1,), (1,)), ((), ())),
        preferred_element_type=F32,
    )
    slot = lax.broadcasted_iota(jnp.int32, (1, CLAT), 1) // LAT_REACH
    outer = (slot == 0) | (slot == 7)
    for a in range(CLON):
        moved = pltpu.roll(added, (7 - 2 * a) * LAT_REACH, 1)
        result32[pl.ds(a, NV, stride=CLON), :] = core[a] + jnp.where(outer, moved, 0.0)
    out[...] = result32[...]


def call(kernel, outs, in_specs, scratch, flops, moved):
    return pl.pallas_call(
        kernel,
        out_shape=[jax.ShapeDtypeStruct(shape, dtype) for shape, dtype in outs],
        in_specs=in_specs,
        out_specs=[VMEM] * len(outs),
        scratch_shapes=scratch,
        compiler_params=pltpu.CompilerParams(vmem_limit_bytes=24 << 20),
        cost_estimate=pl.CostEstimate(flops=flops, bytes_accessed=moved, transcendentals=0),
    )


def in_hbm(array):
    return pltpu.with_memory_space_constraint(array, pltpu.HBM)


def swap(block, axis, first, wraps):
    n = lax.axis_size(axis)
    pairs = [(k, ((k - first) ^ 1) + first) for k in range(n)]
    pairs = [(k, to % n) for k, to in pairs if wraps or 0 <= to < n]
    return lax.ppermute(block, axis, pairs)


def per_device(fine_members, coarse_members, increments, level_weights):
    shapes = ((128, CLAT), (256, CLAT), (128, CLAT))
    own, off_chip, on_chip = call(
        pack_kernel,
        [((512, CLAT), BF16), ((SENT, CLAT), BF16), ((SENT, CLAT), BF16)],
        [pl.BlockSpec(memory_space=pltpu.HBM)] * 3,
        [pltpu.VMEM(shape, BF16) for shape in shapes]
        + [pltpu.VMEM(shape, F32) for shape in shapes]
        + [pltpu.SemaphoreType.DMA((3,))],
        1 << 20,
        1 << 19,
    )(
        in_hbm(fine_members.reshape(KF * CLON, CLAT)),
        in_hbm(coarse_members.reshape(KC * 2, CLAT)),
        in_hbm(increments.reshape(NV * CLON, CLAT)),
    )
    off_chip = swap(off_chip, "lon", 1, True)
    on_chip = swap(on_chip, "lon", 0, True)
    near, far = call(
        edge_kernel,
        [((EDGE, CLAT), BF16), ((EDGE, CLAT), BF16)],
        [VMEM] * 3,
        [],
        1 << 20,
        1 << 19,
    )(off_chip, own, on_chip)
    near = swap(near, "lat", 0, False)
    far = swap(far, "lat", 1, False)
    core, edges, rims = call(
        core_kernel,
        [
            ((CLON, NV, CLAT), F32),
            ((CLAT, KX), BF16),
            ((CLAT, 4 * CLAT), F32),
        ],
        [SMEM] + [VMEM] * 3,
        [
            pltpu.VMEM((KX, 10 * CLAT), BF16),
            pltpu.VMEM((KX, CLON * CLAT), BF16),
            pltpu.VMEM((NV, 10 * CLAT), BF16),
            pltpu.VMEM((LON_REACH + 1, CLAT, CLAT), F32),
        ],
        200 << 20,
        4 << 20,
    )(level_weights, off_chip, own, on_chip)
    (out,) = call(
        rim_kernel,
        [((NV * CLON, CLAT), F32)],
        [VMEM] * 5,
        [pltpu.VMEM((NV * CLON, CLAT), F32)],
        8 << 20,
        1 << 19,
    )(core, edges, rims, near, far)
    return out.reshape(NV, CLON, CLAT)


def solution(mesh):
    in_specs = (P(None, "lon", "lat"), P(None, "lon", "lat"), P(None, "lon", "lat"), P())
    out_specs = P(None, "lon", "lat")
    return jax.shard_map(
        per_device, mesh=mesh, in_specs=in_specs, out_specs=out_specs, check_vma=False
    )
```

```python
import jax
import jax.numpy as jnp
from jax import lax
from jax.experimental import pallas as pl
from jax.experimental.pallas import tpu as pltpu
from jax.sharding import PartitionSpec as P

KF, KC, NV = 32, 128, 32
CLON, CLAT = 4, 128
LON_REACH, LAT_REACH = 3, 16
FV = KF + NV
KX = KF + KC + KF
SENT = 3 * FV + 2 * KC
EDGE = KC + FV
COLUMNS = range(1, 11)
VMEM = pl.BlockSpec(memory_space=pltpu.VMEM)
SMEM = pl.BlockSpec(memory_space=pltpu.SMEM)
F32, BF16 = jnp.float32, jnp.bfloat16

OWN_FV = (0, 64, 128, 448)
OWN_C = (192, 320)
WEST_FV = (None, 0, 64, 384)
WEST_C = (128, 256)
EAST_FV = (0, 64, 128, None)
EAST_C = (192, 320)


def lon_weight(distance):
    return 1.0 - 0.75 * (distance / LON_REACH) ** 2


class Hood:
    def __init__(self, off_chip, own, on_chip):
        self.off_chip, self.own, self.on_chip = off_chip, own, on_chip
        self.odd = lax.axis_index("lon") % 2 == 1

    def rows(self, tile, at, count):
        if tile == 1:
            return self.own[at : at + count, :]
        off, on = self.off_chip[at : at + count, :], self.on_chip[at : at + count, :]
        return jnp.where(self.odd, on, off) if tile == 0 else jnp.where(self.odd, off, on)

    def fv(self, column):
        tile, at = divmod(column, CLON)
        return self.rows(tile, (WEST_FV, OWN_FV, EAST_FV)[tile][at], FV)

    def coarse(self, column):
        tile, at = divmod(column, 2)
        return self.rows(tile, (WEST_C, OWN_C, EAST_C)[tile][at], KC)


def pack_kernel(
    fine, coarse, vectors, own, off_chip, on_chip, fine16, coarse16, vectors16, fine32, coarse32, vectors32, sem
):
    pairs = ((fine, fine16), (coarse, coarse16), (vectors, vectors16))
    copies = [pltpu.make_async_copy(src, dst, sem.at[n]) for n, (src, dst) in enumerate(pairs)]
    for copy in copies:
        copy.start()
    odd = lax.axis_index("lon") % 2 == 1

    def put(block, at):
        own[at : at + block.shape[0], :] = block

    copies[0].wait()
    fine32[...] = fine16[...].astype(F32)
    for a in range(CLON):
        put(fine32[pl.ds(a, KF, stride=CLON), :].astype(BF16), OWN_FV[a])
    copies[1].wait()
    coarse32[...] = coarse16[...].astype(F32)
    for m in range(2):
        put(coarse32[pl.ds(m, KC, stride=2), :].astype(BF16), OWN_C[m])
    copies[2].wait()
    vectors32[...] = vectors16[...].astype(F32)
    for a in range(CLON):
        put(vectors32[pl.ds(a, NV, stride=CLON), :].astype(BF16), OWN_FV[a] + KF)
    to_west, to_east = own[:SENT, :], own[FV:, :]
    off_chip[...] = jnp.where(odd, to_east, to_west)
    on_chip[...] = jnp.where(odd, to_west, to_east)


def edge_kernel(off_chip, own, on_chip, near, far):
    hood = Hood(off_chip, own, on_chip)
    odd = lax.axis_index("lat") % 2 == 1
    lane = lax.broadcasted_iota(jnp.int32, (1, CLAT), 1) // LAT_REACH

    def gather(blocks, at):
        high = jnp.zeros((FV, CLAT), F32)
        low = jnp.zeros((FV, CLAT), F32)
        for slot, block in blocks.items():
            shift = (slot + 1) % 8 * LAT_REACH
            block = block.astype(F32)
            moved = pltpu.roll(block, shift, 1) if shift else block
            high = jnp.where(lane == slot, moved, high)
            low = jnp.where(lane == (slot + 1) % 8, moved, low)
        near[at : at + FV, :] = jnp.where(odd, low, high).astype(BF16)
        far[at : at + FV, :] = jnp.where(odd, high, low).astype(BF16)

    even = {m: hood.fv(2 * m) for m in range(1, 6)}
    uneven = {m: hood.fv(2 * m + 1) for m in range(0, 5)}
    coarse = {m: hood.coarse(m) for m in range(6)}
    upper = {m: block[:FV] for m, block in coarse.items()}
    upper.update({6: even[3], 7: even[4]})
    gather(upper, 0)
    gather({m: block[FV:] for m, block in coarse.items()}, FV)
    gather({**uneven, 5: even[5], 6: even[1], 7: even[2]}, KC)


def anomaly_rows(fine, refined):
    fine = fine - jnp.mean(fine, axis=0, keepdims=True)
    coarse = refined - jnp.mean(refined, axis=0, keepdims=True)
    paired = refined[:KF]
    paired = paired - jnp.mean(paired, axis=0, keepdims=True)
    return fine, coarse, paired


def rim_taper(is_above, parity):
    above = is_above.astype(jnp.int32)
    row = lax.broadcasted_iota(jnp.int32, (CLAT, CLAT), 0)
    lane = lax.broadcasted_iota(jnp.int32, (CLAT, CLAT), 1)
    column = 2 * (lane // LAT_REACH - above) + parity
    lon_gap = jnp.abs(column - CLON - row // (2 * LAT_REACH))
    shift = lane % LAT_REACH - row % LAT_REACH
    lat_gap = LAT_REACH + (2 * above - 1) * shift
    lon_ratio = lon_gap.astype(F32) * (1.0 / LON_REACH)
    lat_ratio = lat_gap.astype(F32) * (1.0 / LAT_REACH)
    here = row // LAT_REACH % 2 + above == 1
    inside = here & (lon_gap <= LON_REACH) & (lat_gap <= LAT_REACH)
    value = (1.0 - 0.75 * lon_ratio * lon_ratio) * (1.0 - 0.75 * lat_ratio * lat_ratio)
    return jnp.where(inside, value, 0.0)


def halfway(values):
    return 0.5 * (values + pltpu.roll(values, CLAT - LAT_REACH, 1))


def rim_terms(rim, edges, taper, is_above):
    refined = rim[:KC].astype(F32)
    coarse = refined - jnp.mean(refined, axis=0, keepdims=True)
    paired = refined[:KF] - jnp.mean(refined[:KF], axis=0, keepdims=True)
    slot = lax.broadcasted_iota(jnp.int32, (1, CLAT), 1) // LAT_REACH
    own_slot = (slot + 8 - is_above.astype(jnp.int32)) % 8
    mixed = rim[KC:].astype(F32)
    even = jnp.where(own_slot <= 2, pltpu.roll(mixed, 3 * LAT_REACH, 1), pltpu.roll(refined[:FV], 5 * LAT_REACH, 1))
    even = jnp.where(own_slot >= 5, mixed, even)
    hood, vectors = [], []
    for values, pair in ((even, (coarse, paired)), (mixed, (halfway(coarse), halfway(paired)))):
        fine = values[:KF] - jnp.mean(values[:KF], axis=0, keepdims=True)
        hood.append(jnp.concatenate([part.astype(BF16) for part in (fine, *pair)], axis=0))
        vectors.append(values[KF:].astype(BF16))
    gram = jnp.dot(edges, jnp.concatenate(hood, axis=1), preferred_element_type=F32)
    added = lax.dot_general(
        jnp.concatenate(vectors, axis=1),
        (taper * gram).astype(BF16),
        (((1,), (1,)), ((), ())),
        preferred_element_type=F32,
    )
    outer = (slot == 0) | (slot == 7)
    return [
        jnp.where(outer, pltpu.roll(added, (7 - 2 * a) * LAT_REACH, 1), 0.0) for a in range(CLON)
    ]


def core_kernel(
    weights, off_chip, own, on_chip, near, out, edges, far_taper, hood, mine, vectors, taper
):
    tiles = Hood(off_chip, own, on_chip)
    i = lax.broadcasted_iota(jnp.int32, (CLAT, CLAT), 0)
    j = lax.broadcasted_iota(jnp.int32, (CLAT, CLAT), 1)
    gap = jnp.abs(i - j)
    ratio = gap.astype(F32) * (1.0 / LAT_REACH)
    band = jnp.where(gap <= LAT_REACH, 1.0 - 0.75 * ratio * ratio, 0.0)
    for distance in range(LON_REACH + 1):
        taper[distance] = band * lon_weight(distance)
    weight_fine = weights[0] * (1.0 / (KF - 1))
    weight_coarse = weights[1] * (1.0 / (KC - 1))
    weight_paired = weights[1] * (-1.0 / (KF - 1))
    lane = lax.broadcasted_iota(jnp.int32, (1, CLAT), 1) // LAT_REACH
    both = jnp.zeros((KX, CLAT), F32)
    coarse_columns = [tiles.coarse(m).astype(F32) for m in range(6)]
    for b in COLUMNS:
        block = tiles.fv(b)
        refined = coarse_columns[b // 2]
        if b % 2:
            refined = 0.5 * (refined + coarse_columns[b // 2 + 1])
        fine, coarse, paired = anomaly_rows(block[:KF].astype(F32), refined)
        lanes = slice((b - 1) * CLAT, b * CLAT)
        hood[:KF, lanes] = fine.astype(BF16)
        hood[KF : KF + KC, lanes] = coarse.astype(BF16)
        hood[KF + KC :, lanes] = paired.astype(BF16)
        vectors[:, lanes] = block[KF:]
        if CLON <= b < 2 * CLON:
            a = b - CLON
            scaled = jnp.concatenate(
                (weight_fine * fine, weight_coarse * coarse, weight_paired * paired), axis=0
            )
            mine[:, a * CLAT : (a + 1) * CLAT] = scaled.astype(BF16)
            moved = pltpu.roll(scaled, (2 * a + 1) * LAT_REACH, 1)
            both = jnp.where(lane // 2 == a, moved, both)
    edges[...] = both.T.astype(BF16)
    odd = lax.axis_index("lat") % 2 == 1
    far_taper[...] = jnp.concatenate([rim_taper(odd, parity) for parity in range(2)], axis=1)
    near_taper = jnp.concatenate([rim_taper(~odd, parity) for parity in range(2)], axis=1)
    near_terms = rim_terms(near[...], edges[...], near_taper, ~odd)
    for a in range(CLON):
        lanes = slice(a * CLAT, (a + 7) * CLAT)
        gram = lax.dot_general(
            mine[:, a * CLAT : (a + 1) * CLAT],
            hood[:, lanes],
            (((0,), (0,)), ((), ())),
            preferred_element_type=F32,
        )
        tapered = jnp.concatenate(
            [
                (taper[abs(n - LON_REACH)] * gram[:, n * CLAT : (n + 1) * CLAT]).astype(BF16)
                for n in range(7)
            ],
            axis=1,
        )
        out[a] = near_terms[a] + lax.dot_general(
            vectors[:, lanes], tapered, (((1,), (1,)), ((), ())), preferred_element_type=F32
        )


def rim_kernel(core, edges, far_taper, far, out):
    odd = lax.axis_index("lat") % 2 == 1
    terms = rim_terms(far[...], edges[...], far_taper[...], odd)
    for a in range(CLON):
        out[pl.ds(a, NV, stride=CLON), :] = core[a] + terms[a]


def call(kernel, outs, in_specs, scratch, flops, moved):
    return pl.pallas_call(
        kernel,
        out_shape=[jax.ShapeDtypeStruct(shape, dtype) for shape, dtype in outs],
        in_specs=in_specs,
        out_specs=[VMEM] * len(outs),
        scratch_shapes=scratch,
        compiler_params=pltpu.CompilerParams(vmem_limit_bytes=24 << 20),
        cost_estimate=pl.CostEstimate(flops=flops, bytes_accessed=moved, transcendentals=0),
    )


def in_hbm(array):
    return pltpu.with_memory_space_constraint(array, pltpu.HBM)


def swap(block, axis, first, wraps):
    n = lax.axis_size(axis)
    pairs = [(k, ((k - first) ^ 1) + first) for k in range(n)]
    pairs = [(k, to % n) for k, to in pairs if wraps or 0 <= to < n]
    return lax.ppermute(block, axis, pairs)


def per_device(fine_members, coarse_members, increments, level_weights):
    shapes = ((128, CLAT), (256, CLAT), (128, CLAT))
    own, off_chip, on_chip = call(
        pack_kernel,
        [((512, CLAT), BF16), ((SENT, CLAT), BF16), ((SENT, CLAT), BF16)],
        [pl.BlockSpec(memory_space=pltpu.HBM)] * 3,
        [pltpu.VMEM(shape, BF16) for shape in shapes]
        + [pltpu.VMEM(shape, F32) for shape in shapes]
        + [pltpu.SemaphoreType.DMA((3,))],
        1 << 20,
        1 << 19,
    )(
        in_hbm(fine_members.reshape(KF * CLON, CLAT)),
        in_hbm(coarse_members.reshape(KC * 2, CLAT)),
        in_hbm(increments.reshape(NV * CLON, CLAT)),
    )
    off_chip = swap(off_chip, "lon", 1, True)
    on_chip = swap(on_chip, "lon", 0, True)
    near, far = call(
        edge_kernel,
        [((EDGE, CLAT), BF16), ((EDGE, CLAT), BF16)],
        [VMEM] * 3,
        [],
        1 << 20,
        1 << 19,
    )(off_chip, own, on_chip)
    near = swap(near, "lat", 0, False)
    far = swap(far, "lat", 1, False)
    core, edges, far_taper = call(
        core_kernel,
        [
            ((CLON, NV, CLAT), F32),
            ((CLAT, KX), BF16),
            ((CLAT, 2 * CLAT), F32),
        ],
        [SMEM] + [VMEM] * 4,
        [
            pltpu.VMEM((KX, 10 * CLAT), BF16),
            pltpu.VMEM((KX, CLON * CLAT), BF16),
            pltpu.VMEM((NV, 10 * CLAT), BF16),
            pltpu.VMEM((LON_REACH + 1, CLAT, CLAT), F32),
        ],
        200 << 20,
        4 << 20,
    )(level_weights, off_chip, own, on_chip, near)
    (out,) = call(
        rim_kernel,
        [((NV * CLON, CLAT), F32)],
        [VMEM] * 4,
        [],
        8 << 20,
        1 << 19,
    )(core, edges, far_taper, far)
    return out.reshape(NV, CLON, CLAT)


def solution(mesh):
    in_specs = (P(None, "lon", "lat"), P(None, "lon", "lat"), P(None, "lon", "lat"), P())
    out_specs = P(None, "lon", "lat")
    return jax.shard_map(
        per_device, mesh=mesh, in_specs=in_specs, out_specs=out_specs, check_vma=False
    )
```

```python
import jax
import jax.numpy as jnp
from jax import lax
from jax.experimental import pallas as pl
from jax.experimental.pallas import tpu as pltpu
from jax.sharding import PartitionSpec as P

KF, KC, NV = 32, 128, 32
CLON, CLAT = 4, 128
LON_REACH, LAT_REACH = 3, 16
FV = KF + NV
KX = KF + KC + KF
SENT = 3 * FV + 2 * KC
TILE = 4 * FV + 2 * KC
PADDED = TILE + 64
EDGE = KC + FV
COLUMNS = range(1, 11)
RING = 16
VMEM = pl.BlockSpec(memory_space=pltpu.VMEM)
F32, BF16 = jnp.float32, jnp.bfloat16

OWN_FV = (0, 64, 128, 448)
OWN_C = (192, 320)
WEST_FV = (None, 0, 64, 384)
WEST_C = (128, 256)
EAST_FV = (0, 64, 128, None)
EAST_C = (192, 320)


def lon_weight(distance):
    return 1.0 - 0.75 * (distance / LON_REACH) ** 2


class Hood:
    def __init__(self, parity, off_chip, own, early, late):
        self.parity, self.off_chip, self.own, self.early, self.late = parity, off_chip, own, early, late
        self.is_early = lax.axis_index("lon") % RING < 2

    def rows(self, tile, at, trimmed_at, count):
        if tile == 1:
            return self.own[at : at + count, :]
        if (tile == 0) == (self.parity == 0):
            return self.off_chip[at : at + count, :]
        late = self.late[trimmed_at : trimmed_at + count, :]
        return jnp.where(self.is_early, self.early[at : at + count, :], late)

    def fv(self, column):
        tile, at = divmod(column, CLON)
        return self.rows(tile, OWN_FV[at], (WEST_FV, OWN_FV, EAST_FV)[tile][at], FV)

    def coarse(self, column):
        tile, at = divmod(column, 2)
        return self.rows(tile, OWN_C[at], (WEST_C, OWN_C, EAST_C)[tile][at], KC)


def pack_kernel(
    fine, coarse, vectors, own, tile, to_east, on_chip, fine16, coarse16, vectors16, fine32, coarse32, vectors32, sem
):
    pairs = ((fine, fine16), (coarse, coarse16), (vectors, vectors16))
    copies = [pltpu.make_async_copy(src, dst, sem.at[n]) for n, (src, dst) in enumerate(pairs)]
    for copy in copies:
        copy.start()
    odd = lax.axis_index("lon") % 2 == 1

    def put(block, at):
        own[at : at + block.shape[0], :] = block

    copies[0].wait()
    fine32[...] = fine16[...].astype(F32)
    for a in range(CLON):
        put(fine32[pl.ds(a, KF, stride=CLON), :].astype(BF16), OWN_FV[a])
    copies[1].wait()
    coarse32[...] = coarse16[...].astype(F32)
    for m in range(2):
        put(coarse32[pl.ds(m, KC, stride=2), :].astype(BF16), OWN_C[m])
    copies[2].wait()
    vectors32[...] = vectors16[...].astype(F32)
    for a in range(CLON):
        put(vectors32[pl.ds(a, NV, stride=CLON), :].astype(BF16), OWN_FV[a] + KF)
    own[TILE:, :] = jnp.zeros((PADDED - TILE, CLAT), BF16)
    tile[...] = own[:TILE, :]
    to_east[...] = own[: TILE + 16, :]
    on_chip[...] = jnp.where(odd, own[:SENT, :], own[FV:TILE, :])


def for_parity(parity, body):
    def kernel(*refs):
        @pl.when(lax.axis_index("lon") % 2 == parity)
        def _():
            body(parity, *refs)

    return kernel


def edge_kernel(parity, off_chip, own, early, late, after, near, far):
    hood = Hood(parity, off_chip, own, early, late)
    odd = lax.axis_index("lat") % 2 == 1
    lane = lax.broadcasted_iota(jnp.int32, (1, CLAT), 1) // LAT_REACH

    def gather(blocks, at):
        high = jnp.zeros((FV, CLAT), F32)
        low = jnp.zeros((FV, CLAT), F32)
        for slot, block in blocks.items():
            shift = (slot + 1) % 8 * LAT_REACH
            block = block.astype(F32)
            moved = pltpu.roll(block, shift, 1) if shift else block
            high = jnp.where(lane == slot, moved, high)
            low = jnp.where(lane == (slot + 1) % 8, moved, low)
        near[at : at + FV, :] = jnp.where(odd, low, high).astype(BF16)
        far[at : at + FV, :] = jnp.where(odd, high, low).astype(BF16)

    even = {m: hood.fv(2 * m) for m in range(1, 6)}
    uneven = {m: hood.fv(2 * m + 1) for m in range(0, 5)}
    coarse = {m: hood.coarse(m) for m in range(6)}
    upper = {m: block[:FV] for m, block in coarse.items()}
    upper.update({6: even[3], 7: even[4]})
    gather(upper, 0)
    gather({m: block[FV:] for m, block in coarse.items()}, FV)
    gather({**uneven, 5: even[5], 6: even[1], 7: even[2]}, KC)


def anomaly_rows(fine, refined):
    fine = fine - jnp.mean(fine, axis=0, keepdims=True)
    coarse = refined - jnp.mean(refined, axis=0, keepdims=True)
    paired = refined[:KF]
    paired = paired - jnp.mean(paired, axis=0, keepdims=True)
    return fine, coarse, paired


def rim_taper(is_above, parity):
    above = is_above.astype(jnp.int32)
    row = lax.broadcasted_iota(jnp.int32, (CLAT, CLAT), 0)
    lane = lax.broadcasted_iota(jnp.int32, (CLAT, CLAT), 1)
    column = 2 * (lane // LAT_REACH - above) + parity
    lon_gap = jnp.abs(column - CLON - row // (2 * LAT_REACH))
    shift = lane % LAT_REACH - row % LAT_REACH
    lat_gap = LAT_REACH + (2 * above - 1) * shift
    lon_ratio = lon_gap.astype(F32) * (1.0 / LON_REACH)
    lat_ratio = lat_gap.astype(F32) * (1.0 / LAT_REACH)
    here = row // LAT_REACH % 2 + above == 1
    inside = here & (lon_gap <= LON_REACH) & (lat_gap <= LAT_REACH)
    value = (1.0 - 0.75 * lon_ratio * lon_ratio) * (1.0 - 0.75 * lat_ratio * lat_ratio)
    return jnp.where(inside, value, 0.0)


def halfway(values):
    return 0.5 * (values + pltpu.roll(values, CLAT - LAT_REACH, 1))


def rim_terms(rim, edges, taper, is_above):
    refined = rim[:KC].astype(F32)
    coarse = refined - jnp.mean(refined, axis=0, keepdims=True)
    paired = refined[:KF] - jnp.mean(refined[:KF], axis=0, keepdims=True)
    slot = lax.broadcasted_iota(jnp.int32, (1, CLAT), 1) // LAT_REACH
    own_slot = (slot + 8 - is_above.astype(jnp.int32)) % 8
    mixed = rim[KC:].astype(F32)
    even = jnp.where(own_slot <= 2, pltpu.roll(mixed, 3 * LAT_REACH, 1), pltpu.roll(refined[:FV], 5 * LAT_REACH, 1))
    even = jnp.where(own_slot >= 5, mixed, even)
    hood, vectors = [], []
    for values, pair in ((even, (coarse, paired)), (mixed, (halfway(coarse), halfway(paired)))):
        fine = values[:KF] - jnp.mean(values[:KF], axis=0, keepdims=True)
        hood.append(jnp.concatenate([part.astype(BF16) for part in (fine, *pair)], axis=0))
        vectors.append(values[KF:].astype(BF16))
    gram = jnp.dot(edges, jnp.concatenate(hood, axis=1), preferred_element_type=F32)
    added = lax.dot_general(
        jnp.concatenate(vectors, axis=1),
        (taper * gram).astype(BF16),
        (((1,), (1,)), ((), ())),
        preferred_element_type=F32,
    )
    outer = (slot == 0) | (slot == 7)
    return [
        jnp.where(outer, pltpu.roll(added, (7 - 2 * a) * LAT_REACH, 1), 0.0) for a in range(CLON)
    ]


def core_kernel(
    parity, weights, off_chip, own, early, late, near, out, edges, far_taper, hood, mine, vectors, taper
):
    tiles = Hood(parity, off_chip, own, early, late)
    i = lax.broadcasted_iota(jnp.int32, (CLAT, CLAT), 0)
    j = lax.broadcasted_iota(jnp.int32, (CLAT, CLAT), 1)
    gap = jnp.abs(i - j)
    ratio = gap.astype(F32) * (1.0 / LAT_REACH)
    band = jnp.where(gap <= LAT_REACH, 1.0 - 0.75 * ratio * ratio, 0.0)
    for distance in range(LON_REACH + 1):
        taper[distance] = band * lon_weight(distance)
    level = weights[...]
    weight_fine = level[:, :1] * (1.0 / (KF - 1))
    weight_coarse = level[:, 1:] * (1.0 / (KC - 1))
    weight_paired = level[:, 1:] * (-1.0 / (KF - 1))
    lane = lax.broadcasted_iota(jnp.int32, (1, CLAT), 1) // LAT_REACH
    both = jnp.zeros((KX, CLAT), F32)
    coarse_columns = [tiles.coarse(m).astype(F32) for m in range(6)]
    for b in COLUMNS:
        block = tiles.fv(b)
        refined = coarse_columns[b // 2]
        if b % 2:
            refined = 0.5 * (refined + coarse_columns[b // 2 + 1])
        fine, coarse, paired = anomaly_rows(block[:KF].astype(F32), refined)
        lanes = slice((b - 1) * CLAT, b * CLAT)
        hood[:KF, lanes] = fine.astype(BF16)
        hood[KF : KF + KC, lanes] = coarse.astype(BF16)
        hood[KF + KC :, lanes] = paired.astype(BF16)
        vectors[:, lanes] = block[KF:]
        if CLON <= b < 2 * CLON:
            a = b - CLON
            scaled = jnp.concatenate(
                (weight_fine * fine, weight_coarse * coarse, weight_paired * paired), axis=0
            )
            mine[:, a * CLAT : (a + 1) * CLAT] = scaled.astype(BF16)
            moved = pltpu.roll(scaled, (2 * a + 1) * LAT_REACH, 1)
            both = jnp.where(lane // 2 == a, moved, both)
    edges[...] = both.T.astype(BF16)
    odd = lax.axis_index("lat") % 2 == 1
    far_taper[...] = jnp.concatenate([rim_taper(odd, n) for n in range(2)], axis=1)
    near_taper = jnp.concatenate([rim_taper(~odd, n) for n in range(2)], axis=1)
    near_terms = rim_terms(near[...], edges[...], near_taper, ~odd)
    for a in range(CLON):
        lanes = slice(a * CLAT, (a + 7) * CLAT)
        gram = lax.dot_general(
            mine[:, a * CLAT : (a + 1) * CLAT],
            hood[:, lanes],
            (((0,), (0,)), ((), ())),
            preferred_element_type=F32,
        )
        tapered = jnp.concatenate(
            [
                (taper[abs(n - LON_REACH)] * gram[:, n * CLAT : (n + 1) * CLAT]).astype(BF16)
                for n in range(7)
            ],
            axis=1,
        )
        out[a] = near_terms[a] + lax.dot_general(
            vectors[:, lanes], tapered, (((1,), (1,)), ((), ())), preferred_element_type=F32
        )


def rim_kernel(parity, core, edges, far_taper, far, out):
    odd = lax.axis_index("lat") % 2 == 1
    terms = rim_terms(far[...], edges[...], far_taper[...], odd)
    for a in range(CLON):
        out[pl.ds(a, NV, stride=CLON), :] = core[a] + terms[a]


def last_kernel(even_out, core, edges, far_taper, far, out):
    odd = lax.axis_index("lon") % 2 == 1

    @pl.when(odd)
    def _():
        rim_kernel(1, core, edges, far_taper, far, out)

    @pl.when(~odd)
    def _():
        out[...] = even_out[...]


def call(kernel, outs, in_specs, scratch, flops, moved):
    return pl.pallas_call(
        kernel,
        out_shape=[jax.ShapeDtypeStruct(shape, dtype) for shape, dtype in outs],
        in_specs=in_specs,
        out_specs=[VMEM] * len(outs),
        scratch_shapes=scratch,
        compiler_params=pltpu.CompilerParams(vmem_limit_bytes=24 << 20),
        cost_estimate=pl.CostEstimate(flops=flops, bytes_accessed=moved, transcendentals=0),
    )


def in_hbm(array):
    return pltpu.with_memory_space_constraint(array, pltpu.HBM)


def partner(k, first):
    return ((k - first) ^ 1) + first


def swap_lat(block, first, parity):
    lon, lat = lax.axis_size("lon"), lax.axis_size("lat")
    pairs = [(k, partner(k, first)) for k in range(lat) if 0 <= partner(k, first) < lat]
    pairs = [(n * lat + k, n * lat + to) for n in range(parity, lon, 2) for k, to in pairs]
    return lax.ppermute(block, ("lon", "lat"), pairs)


def send_lon(block, first, chosen):
    n = lax.axis_size("lon")
    return lax.ppermute(block, "lon", [(k, partner(k, first) % n) for k in range(n) if chosen(k)])


def per_device(fine_members, coarse_members, increments, level_weights):
    shapes = ((128, CLAT), (256, CLAT), (128, CLAT))
    own, tile, to_east, on_chip = call(
        pack_kernel,
        [((PADDED, CLAT), BF16), ((TILE, CLAT), BF16), ((TILE + 16, CLAT), BF16), ((SENT, CLAT), BF16)],
        [pl.BlockSpec(memory_space=pltpu.HBM)] * 3,
        [pltpu.VMEM(shape, BF16) for shape in shapes]
        + [pltpu.VMEM(shape, F32) for shape in shapes]
        + [pltpu.SemaphoreType.DMA((3,))],
        1 << 20,
        1 << 19,
    )(
        in_hbm(fine_members.reshape(KF * CLON, CLAT)),
        in_hbm(coarse_members.reshape(KC * 2, CLAT)),
        in_hbm(increments.reshape(NV * CLON, CLAT)),
    )
    from_west = send_lon(to_east, 1, lambda k: k % 2 == 1)
    early = send_lon(tile, 0, lambda k: k % RING < 2)
    from_east = send_lon(own, 1, lambda k: k % 2 == 0)
    late = send_lon(on_chip, 0, lambda k: k % RING >= 2)
    cores, after = [], own
    for parity, received in ((0, from_west), (1, from_east)):
        near, far = call(
            for_parity(parity, edge_kernel),
            [((EDGE, CLAT), BF16), ((EDGE, CLAT), BF16)],
            [VMEM] * 5,
            [],
            1,
            1,
        )(received, own, early, late, after)
        after = near
        near = swap_lat(near, 0, parity)
        far = swap_lat(far, 1, parity)
        core = call(
            for_parity(parity, core_kernel),
            [
                ((CLON, NV, CLAT), F32),
                ((CLAT, KX), BF16),
                ((CLAT, 2 * CLAT), F32),
            ],
            [VMEM] * 6,
            [
                pltpu.VMEM((KX, 10 * CLAT), BF16),
                pltpu.VMEM((KX, CLON * CLAT), BF16),
                pltpu.VMEM((NV, 10 * CLAT), BF16),
                pltpu.VMEM((LON_REACH + 1, CLAT, CLAT), F32),
            ],
            200 << 20,
            4 << 20,
        )(level_weights.reshape(1, 2), received, own, early, late, near)
        cores.append((*core, far))
    result = ((NV * CLON, CLAT), F32)
    (even_out,) = call(for_parity(0, rim_kernel), [result], [VMEM] * 4, [], 8 << 20, 1 << 19)(*cores[0])
    (out,) = call(last_kernel, [result], [VMEM] * 5, [], 8 << 20, 1 << 19)(even_out, *cores[1])
    return out.reshape(NV, CLON, CLAT)


def solution(mesh):
    in_specs = (P(None, "lon", "lat"), P(None, "lon", "lat"), P(None, "lon", "lat"), P())
    out_specs = P(None, "lon", "lat")
    return jax.shard_map(
        per_device, mesh=mesh, in_specs=in_specs, out_specs=out_specs, check_vma=False
    )
```

```python
import jax
import jax.numpy as jnp
from jax import lax
from jax.experimental import pallas as pl
from jax.experimental.pallas import tpu as pltpu
from jax.sharding import PartitionSpec as P

KF, KC, NV = 32, 128, 32
CLON, CLAT = 4, 128
LON_REACH, LAT_REACH = 3, 16
FV = KF + NV
KX = KF + KC + KF
SENT = 3 * FV + 2 * KC
TILE = 4 * FV + 2 * KC
PADDED, EASTWARD, EARLY = 544, 480, 464
EDGE = KC + FV
COLUMNS = range(1, 11)
RING = 16
VMEM = pl.BlockSpec(memory_space=pltpu.VMEM)
F32, BF16 = jnp.float32, jnp.bfloat16

OWN_FV = (0, 64, 128, 448)
OWN_C = (192, 320)
WEST_FV = (None, 0, 64, 384)
WEST_C = (128, 256)
EAST_FV = (0, 64, 128, None)
EAST_C = (192, 320)


def lon_weight(distance):
    return 1.0 - 0.75 * (distance / LON_REACH) ** 2


class Hood:
    def __init__(self, parity, off_chip, own, early, late):
        self.parity, self.off_chip, self.own, self.early, self.late = parity, off_chip, own, early, late
        self.is_early = lax.axis_index("lon") % RING < 2

    def rows(self, tile, at, count):
        if tile == 1:
            return self.own[at : at + count, :]
        if (tile == 0) == (self.parity == 0):
            return self.off_chip[at : at + count, :]
        early, late = self.early[at : at + count, :], self.late[at : at + count, :]
        return jnp.where(self.is_early, early, late)

    def fv(self, column):
        tile, at = divmod(column, CLON)
        return self.rows(tile, (WEST_FV, OWN_FV, EAST_FV)[tile][at], FV)

    def coarse(self, column):
        tile, at = divmod(column, 2)
        return self.rows(tile, (WEST_C, OWN_C, EAST_C)[tile][at], KC)


def pack_kernel(
    fine, coarse, vectors, own, to_east, early, on_chip, fine16, coarse16, vectors16, fine32, coarse32, vectors32, sem
):
    pairs = ((fine, fine16), (coarse, coarse16), (vectors, vectors16))
    copies = [pltpu.make_async_copy(src, dst, sem.at[n]) for n, (src, dst) in enumerate(pairs)]
    for copy in copies:
        copy.start()
    odd = lax.axis_index("lon") % 2 == 1

    def put(block, at):
        own[at : at + block.shape[0], :] = block

    copies[0].wait()
    fine32[...] = fine16[...].astype(F32)
    for a in range(CLON):
        put(fine32[pl.ds(a, KF, stride=CLON), :].astype(BF16), OWN_FV[a])
    copies[1].wait()
    coarse32[...] = coarse16[...].astype(F32)
    for m in range(2):
        put(coarse32[pl.ds(m, KC, stride=2), :].astype(BF16), OWN_C[m])
    copies[2].wait()
    vectors32[...] = vectors16[...].astype(F32)
    for a in range(CLON):
        put(vectors32[pl.ds(a, NV, stride=CLON), :].astype(BF16), OWN_FV[a] + KF)
    own[TILE:, :] = jnp.zeros((PADDED - TILE, CLAT), BF16)
    to_east[:SENT, :] = own[FV:TILE, :]
    to_east[SENT:, :] = jnp.zeros((EASTWARD - SENT, CLAT), BF16)
    trimmed = jnp.where(odd, own[:SENT, :], own[FV:TILE, :])
    early[:SENT, :] = trimmed
    early[SENT:, :] = jnp.zeros((EARLY - SENT, CLAT), BF16)
    on_chip[...] = trimmed


def for_parity(parity, body):
    def kernel(*refs):
        @pl.when(lax.axis_index("lon") % 2 == parity)
        def _():
            body(parity, *refs)

    return kernel


def edge_kernel(parity, off_chip, own, early, late, after, near, far):
    hood = Hood(parity, off_chip, own, early, late)
    odd = lax.axis_index("lat") % 2 == 1
    lane = lax.broadcasted_iota(jnp.int32, (1, CLAT), 1) // LAT_REACH

    def gather(blocks, at):
        high = jnp.zeros((FV, CLAT), F32)
        low = jnp.zeros((FV, CLAT), F32)
        for slot, block in blocks.items():
            shift = (slot + 1) % 8 * LAT_REACH
            block = block.astype(F32)
            moved = pltpu.roll(block, shift, 1) if shift else block
            high = jnp.where(lane == slot, moved, high)
            low = jnp.where(lane == (slot + 1) % 8, moved, low)
        near[at : at + FV, :] = jnp.where(odd, low, high).astype(BF16)
        far[at : at + FV, :] = jnp.where(odd, high, low).astype(BF16)

    even = {m: hood.fv(2 * m) for m in range(1, 6)}
    uneven = {m: hood.fv(2 * m + 1) for m in range(0, 5)}
    coarse = {m: hood.coarse(m) for m in range(6)}
    upper = {m: block[:FV] for m, block in coarse.items()}
    upper.update({6: even[3], 7: even[4]})
    gather(upper, 0)
    gather({m: block[FV:] for m, block in coarse.items()}, FV)
    gather({**uneven, 5: even[5], 6: even[1], 7: even[2]}, KC)


def anomaly_rows(fine, refined):
    fine = fine - jnp.mean(fine, axis=0, keepdims=True)
    coarse = refined - jnp.mean(refined, axis=0, keepdims=True)
    paired = refined[:KF]
    paired = paired - jnp.mean(paired, axis=0, keepdims=True)
    return fine, coarse, paired


def rim_taper(is_above, parity):
    above = is_above.astype(jnp.int32)
    row = lax.broadcasted_iota(jnp.int32, (CLAT, CLAT), 0)
    lane = lax.broadcasted_iota(jnp.int32, (CLAT, CLAT), 1)
    column = 2 * (lane // LAT_REACH - above) + parity
    lon_gap = jnp.abs(column - CLON - row // (2 * LAT_REACH))
    shift = lane % LAT_REACH - row % LAT_REACH
    lat_gap = LAT_REACH + (2 * above - 1) * shift
    lon_ratio = lon_gap.astype(F32) * (1.0 / LON_REACH)
    lat_ratio = lat_gap.astype(F32) * (1.0 / LAT_REACH)
    here = row // LAT_REACH % 2 + above == 1
    inside = here & (lon_gap <= LON_REACH) & (lat_gap <= LAT_REACH)
    value = (1.0 - 0.75 * lon_ratio * lon_ratio) * (1.0 - 0.75 * lat_ratio * lat_ratio)
    return jnp.where(inside, value, 0.0)


def halfway(values):
    return 0.5 * (values + pltpu.roll(values, CLAT - LAT_REACH, 1))


def rim_terms(rim, edges, taper, is_above):
    refined = rim[:KC].astype(F32)
    coarse = refined - jnp.mean(refined, axis=0, keepdims=True)
    paired = refined[:KF] - jnp.mean(refined[:KF], axis=0, keepdims=True)
    slot = lax.broadcasted_iota(jnp.int32, (1, CLAT), 1) // LAT_REACH
    own_slot = (slot + 8 - is_above.astype(jnp.int32)) % 8
    mixed = rim[KC:].astype(F32)
    even = jnp.where(own_slot <= 2, pltpu.roll(mixed, 3 * LAT_REACH, 1), pltpu.roll(refined[:FV], 5 * LAT_REACH, 1))
    even = jnp.where(own_slot >= 5, mixed, even)
    hood, vectors = [], []
    for values, pair in ((even, (coarse, paired)), (mixed, (halfway(coarse), halfway(paired)))):
        fine = values[:KF] - jnp.mean(values[:KF], axis=0, keepdims=True)
        hood.append(jnp.concatenate([part.astype(BF16) for part in (fine, *pair)], axis=0))
        vectors.append(values[KF:].astype(BF16))
    gram = jnp.dot(edges, jnp.concatenate(hood, axis=1), preferred_element_type=F32)
    added = lax.dot_general(
        jnp.concatenate(vectors, axis=1),
        (taper * gram).astype(BF16),
        (((1,), (1,)), ((), ())),
        preferred_element_type=F32,
    )
    outer = (slot == 0) | (slot == 7)
    return [
        jnp.where(outer, pltpu.roll(added, (7 - 2 * a) * LAT_REACH, 1), 0.0) for a in range(CLON)
    ]


def core_kernel(
    parity, weights, off_chip, own, early, late, near, out, edges, far_taper, hood, mine, vectors, taper
):
    tiles = Hood(parity, off_chip, own, early, late)
    i = lax.broadcasted_iota(jnp.int32, (CLAT, CLAT), 0)
    j = lax.broadcasted_iota(jnp.int32, (CLAT, CLAT), 1)
    gap = jnp.abs(i - j)
    ratio = gap.astype(F32) * (1.0 / LAT_REACH)
    band = jnp.where(gap <= LAT_REACH, 1.0 - 0.75 * ratio * ratio, 0.0)
    for distance in range(LON_REACH + 1):
        taper[distance] = band * lon_weight(distance)
    level = weights[...]
    weight_fine = level[:, :1] * (1.0 / (KF - 1))
    weight_coarse = level[:, 1:] * (1.0 / (KC - 1))
    weight_paired = level[:, 1:] * (-1.0 / (KF - 1))
    lane = lax.broadcasted_iota(jnp.int32, (1, CLAT), 1) // LAT_REACH
    both = jnp.zeros((KX, CLAT), F32)
    coarse_columns = [tiles.coarse(m).astype(F32) for m in range(6)]
    for b in COLUMNS:
        block = tiles.fv(b)
        refined = coarse_columns[b // 2]
        if b % 2:
            refined = 0.5 * (refined + coarse_columns[b // 2 + 1])
        fine, coarse, paired = anomaly_rows(block[:KF].astype(F32), refined)
        lanes = slice((b - 1) * CLAT, b * CLAT)
        hood[:KF, lanes] = fine.astype(BF16)
        hood[KF : KF + KC, lanes] = coarse.astype(BF16)
        hood[KF + KC :, lanes] = paired.astype(BF16)
        vectors[:, lanes] = block[KF:]
        if CLON <= b < 2 * CLON:
            a = b - CLON
            scaled = jnp.concatenate(
                (weight_fine * fine, weight_coarse * coarse, weight_paired * paired), axis=0
            )
            mine[:, a * CLAT : (a + 1) * CLAT] = scaled.astype(BF16)
            moved = pltpu.roll(scaled, (2 * a + 1) * LAT_REACH, 1)
            both = jnp.where(lane // 2 == a, moved, both)
    edges[...] = both.T.astype(BF16)
    odd = lax.axis_index("lat") % 2 == 1
    far_taper[...] = jnp.concatenate([rim_taper(odd, n) for n in range(2)], axis=1)
    near_taper = jnp.concatenate([rim_taper(~odd, n) for n in range(2)], axis=1)
    near_terms = rim_terms(near[...], edges[...], near_taper, ~odd)
    for a in range(CLON):
        lanes = slice(a * CLAT, (a + 7) * CLAT)
        gram = lax.dot_general(
            mine[:, a * CLAT : (a + 1) * CLAT],
            hood[:, lanes],
            (((0,), (0,)), ((), ())),
            preferred_element_type=F32,
        )
        tapered = jnp.concatenate(
            [
                (taper[abs(n - LON_REACH)] * gram[:, n * CLAT : (n + 1) * CLAT]).astype(BF16)
                for n in range(7)
            ],
            axis=1,
        )
        out[a] = near_terms[a] + lax.dot_general(
            vectors[:, lanes], tapered, (((1,), (1,)), ((), ())), preferred_element_type=F32
        )


def rim_kernel(parity, core, edges, far_taper, far, out):
    odd = lax.axis_index("lat") % 2 == 1
    terms = rim_terms(far[...], edges[...], far_taper[...], odd)
    for a in range(CLON):
        out[pl.ds(a, NV, stride=CLON), :] = core[a] + terms[a]


def last_kernel(even_out, core, edges, far_taper, far, out):
    odd = lax.axis_index("lon") % 2 == 1

    @pl.when(odd)
    def _():
        rim_kernel(1, core, edges, far_taper, far, out)

    @pl.when(~odd)
    def _():
        out[...] = even_out[...]


def call(kernel, outs, in_specs, scratch, flops, moved):
    return pl.pallas_call(
        kernel,
        out_shape=[jax.ShapeDtypeStruct(shape, dtype) for shape, dtype in outs],
        in_specs=in_specs,
        out_specs=[VMEM] * len(outs),
        scratch_shapes=scratch,
        compiler_params=pltpu.CompilerParams(vmem_limit_bytes=24 << 20),
        cost_estimate=pl.CostEstimate(flops=flops, bytes_accessed=moved, transcendentals=0),
    )


def in_hbm(array):
    return pltpu.with_memory_space_constraint(array, pltpu.HBM)


def partner(k, first):
    return ((k - first) ^ 1) + first


def swap_lat(block, first, parity):
    lon, lat = lax.axis_size("lon"), lax.axis_size("lat")
    pairs = [(k, partner(k, first)) for k in range(lat) if 0 <= partner(k, first) < lat]
    pairs = [(n * lat + k, n * lat + to) for n in range(parity, lon, 2) for k, to in pairs]
    return lax.ppermute(block, ("lon", "lat"), pairs)


def send_lon(block, first, chosen):
    n = lax.axis_size("lon")
    return lax.ppermute(block, "lon", [(k, partner(k, first) % n) for k in range(n) if chosen(k)])


def per_device(fine_members, coarse_members, increments, level_weights):
    shapes = ((128, CLAT), (256, CLAT), (128, CLAT))
    own, to_east, early, on_chip = call(
        pack_kernel,
        [((rows, CLAT), BF16) for rows in (PADDED, EASTWARD, EARLY, SENT)],
        [pl.BlockSpec(memory_space=pltpu.HBM)] * 3,
        [pltpu.VMEM(shape, BF16) for shape in shapes]
        + [pltpu.VMEM(shape, F32) for shape in shapes]
        + [pltpu.SemaphoreType.DMA((3,))],
        1 << 20,
        1 << 19,
    )(
        in_hbm(fine_members.reshape(KF * CLON, CLAT)),
        in_hbm(coarse_members.reshape(KC * 2, CLAT)),
        in_hbm(increments.reshape(NV * CLON, CLAT)),
    )
    from_west = send_lon(to_east, 1, lambda k: k % 2 == 1)
    early = send_lon(early, 0, lambda k: k % RING < 2)
    from_east = send_lon(own, 1, lambda k: k % 2 == 0)
    late = send_lon(on_chip, 0, lambda k: k % RING >= 2)
    cores, after = [], own
    for parity, received in ((0, from_west), (1, from_east)):
        near, far = call(
            for_parity(parity, edge_kernel),
            [((EDGE, CLAT), BF16), ((EDGE, CLAT), BF16)],
            [VMEM] * 5,
            [],
            1,
            1,
        )(received, own, early, late, after)
        after = near
        near = swap_lat(near, 0, parity)
        far = swap_lat(far, 1, parity)
        core = call(
            for_parity(parity, core_kernel),
            [
                ((CLON, NV, CLAT), F32),
                ((CLAT, KX), BF16),
                ((CLAT, 2 * CLAT), F32),
            ],
            [VMEM] * 6,
            [
                pltpu.VMEM((KX, 10 * CLAT), BF16),
                pltpu.VMEM((KX, CLON * CLAT), BF16),
                pltpu.VMEM((NV, 10 * CLAT), BF16),
                pltpu.VMEM((LON_REACH + 1, CLAT, CLAT), F32),
            ],
            200 << 20,
            4 << 20,
        )(level_weights.reshape(1, 2), received, own, early, late, near)
        cores.append((*core, far))
    result = ((NV * CLON, CLAT), F32)
    (even_out,) = call(for_parity(0, rim_kernel), [result], [VMEM] * 4, [], 8 << 20, 1 << 19)(*cores[0])
    (out,) = call(last_kernel, [result], [VMEM] * 5, [], 8 << 20, 1 << 19)(even_out, *cores[1])
    return out.reshape(NV, CLON, CLAT)


def solution(mesh):
    in_specs = (P(None, "lon", "lat"), P(None, "lon", "lat"), P(None, "lon", "lat"), P())
    out_specs = P(None, "lon", "lat")
    return jax.shard_map(
        per_device, mesh=mesh, in_specs=in_specs, out_specs=out_specs, check_vma=False
    )
```

```python
import jax
import jax.numpy as jnp
from jax import lax
from jax.experimental import pallas as pl
from jax.experimental.pallas import tpu as pltpu
from jax.sharding import PartitionSpec as P

KF, KC, NV = 32, 128, 32
CLON, CLAT = 4, 128
LON_REACH, LAT_REACH = 3, 16
FV = KF + NV
KX = KF + KC + KF
SENT = 3 * FV + 2 * KC
TILE = 4 * FV + 2 * KC
PADDED, EASTWARD, EARLY = 536, 472, 464
EDGE = KC + FV
COLUMNS = range(1, 11)
RING = 16
VMEM = pl.BlockSpec(memory_space=pltpu.VMEM)
F32, BF16 = jnp.float32, jnp.bfloat16

OWN_FV = (0, 64, 128, 448)
OWN_C = (192, 320)
WEST_FV = (None, 0, 64, 384)
WEST_C = (128, 256)
EAST_FV = (0, 64, 128, None)
EAST_C = (192, 320)


def lon_weight(distance):
    return 1.0 - 0.75 * (distance / LON_REACH) ** 2


class Hood:
    def __init__(self, parity, off_chip, own, early, late):
        self.parity, self.off_chip, self.own, self.early, self.late = parity, off_chip, own, early, late
        self.is_early = lax.axis_index("lon") % RING < 2

    def rows(self, tile, at, count):
        if tile == 1:
            return self.own[at : at + count, :]
        if (tile == 0) == (self.parity == 0):
            return self.off_chip[at : at + count, :]
        early, late = self.early[at : at + count, :], self.late[at : at + count, :]
        return jnp.where(self.is_early, early, late)

    def fv(self, column):
        tile, at = divmod(column, CLON)
        return self.rows(tile, (WEST_FV, OWN_FV, EAST_FV)[tile][at], FV)

    def coarse(self, column):
        tile, at = divmod(column, 2)
        return self.rows(tile, (WEST_C, OWN_C, EAST_C)[tile][at], KC)


def pack_kernel(
    fine, coarse, vectors, own, to_east, early, on_chip, fine16, coarse16, vectors16, fine32, coarse32, vectors32, sem
):
    half = KC
    pairs = (
        (fine, fine16),
        (coarse.at[:half], coarse16.at[:half]),
        (coarse.at[half:], coarse16.at[half:]),
        (vectors, vectors16),
    )
    copies = [pltpu.make_async_copy(src, dst, sem.at[n]) for n, (src, dst) in enumerate(pairs)]
    for copy in copies:
        copy.start()
    odd = lax.axis_index("lon") % 2 == 1

    def put(block, at):
        own[at : at + block.shape[0], :] = block

    copies[0].wait()
    fine32[...] = fine16[...].astype(F32)
    for a in range(CLON):
        put(fine32[pl.ds(a, KF, stride=CLON), :].astype(BF16), OWN_FV[a])
    copies[1].wait()
    copies[2].wait()
    coarse32[...] = coarse16[...].astype(F32)
    for m in range(2):
        put(coarse32[pl.ds(m, KC, stride=2), :].astype(BF16), OWN_C[m])
    copies[3].wait()
    vectors32[...] = vectors16[...].astype(F32)
    for a in range(CLON):
        put(vectors32[pl.ds(a, NV, stride=CLON), :].astype(BF16), OWN_FV[a] + KF)
    own[TILE:, :] = jnp.zeros((PADDED - TILE, CLAT), BF16)
    to_east[:SENT, :] = own[FV:TILE, :]
    to_east[SENT:, :] = jnp.zeros((EASTWARD - SENT, CLAT), BF16)
    trimmed = jnp.where(odd, own[:SENT, :], own[FV:TILE, :])
    early[:SENT, :] = trimmed
    early[SENT:, :] = jnp.zeros((EARLY - SENT, CLAT), BF16)
    on_chip[...] = trimmed


def for_parity(parity, body):
    def kernel(*refs):
        @pl.when(lax.axis_index("lon") % 2 == parity)
        def _():
            body(parity, *refs)

    return kernel


def edge_kernel(parity, off_chip, own, early, late, after, near, far):
    hood = Hood(parity, off_chip, own, early, late)
    odd = lax.axis_index("lat") % 2 == 1
    lane = lax.broadcasted_iota(jnp.int32, (1, CLAT), 1) // LAT_REACH

    def gather(blocks, at):
        high = jnp.zeros((FV, CLAT), F32)
        low = jnp.zeros((FV, CLAT), F32)
        for slot, block in blocks.items():
            shift = (slot + 1) % 8 * LAT_REACH
            block = block.astype(F32)
            moved = pltpu.roll(block, shift, 1) if shift else block
            high = jnp.where(lane == slot, moved, high)
            low = jnp.where(lane == (slot + 1) % 8, moved, low)
        near[at : at + FV, :] = jnp.where(odd, low, high).astype(BF16)
        far[at : at + FV, :] = jnp.where(odd, high, low).astype(BF16)

    even = {m: hood.fv(2 * m) for m in range(1, 6)}
    uneven = {m: hood.fv(2 * m + 1) for m in range(0, 5)}
    coarse = {m: hood.coarse(m) for m in range(6)}
    upper = {m: block[:FV] for m, block in coarse.items()}
    upper.update({6: even[3], 7: even[4]})
    gather(upper, 0)
    gather({m: block[FV:] for m, block in coarse.items()}, FV)
    gather({**uneven, 5: even[5], 6: even[1], 7: even[2]}, KC)


def anomaly_rows(fine, refined):
    fine = fine - jnp.mean(fine, axis=0, keepdims=True)
    coarse = refined - jnp.mean(refined, axis=0, keepdims=True)
    paired = refined[:KF]
    paired = paired - jnp.mean(paired, axis=0, keepdims=True)
    return fine, coarse, paired


def rim_taper(is_above, parity):
    above = is_above.astype(jnp.int32)
    row = lax.broadcasted_iota(jnp.int32, (CLAT, CLAT), 0)
    lane = lax.broadcasted_iota(jnp.int32, (CLAT, CLAT), 1)
    column = 2 * (lane // LAT_REACH - above) + parity
    lon_gap = jnp.abs(column - CLON - row // (2 * LAT_REACH))
    shift = lane % LAT_REACH - row % LAT_REACH
    lat_gap = LAT_REACH + (2 * above - 1) * shift
    lon_ratio = lon_gap.astype(F32) * (1.0 / LON_REACH)
    lat_ratio = lat_gap.astype(F32) * (1.0 / LAT_REACH)
    here = row // LAT_REACH % 2 + above == 1
    inside = here & (lon_gap <= LON_REACH) & (lat_gap <= LAT_REACH)
    value = (1.0 - 0.75 * lon_ratio * lon_ratio) * (1.0 - 0.75 * lat_ratio * lat_ratio)
    return jnp.where(inside, value, 0.0)


def halfway(values):
    return 0.5 * (values + pltpu.roll(values, CLAT - LAT_REACH, 1))


def rim_terms(rim, edges, taper, is_above):
    refined = rim[:KC].astype(F32)
    coarse = refined - jnp.mean(refined, axis=0, keepdims=True)
    paired = refined[:KF] - jnp.mean(refined[:KF], axis=0, keepdims=True)
    slot = lax.broadcasted_iota(jnp.int32, (1, CLAT), 1) // LAT_REACH
    own_slot = (slot + 8 - is_above.astype(jnp.int32)) % 8
    mixed = rim[KC:].astype(F32)
    even = jnp.where(own_slot <= 2, pltpu.roll(mixed, 3 * LAT_REACH, 1), pltpu.roll(refined[:FV], 5 * LAT_REACH, 1))
    even = jnp.where(own_slot >= 5, mixed, even)
    hood, vectors = [], []
    for values, pair in ((even, (coarse, paired)), (mixed, (halfway(coarse), halfway(paired)))):
        fine = values[:KF] - jnp.mean(values[:KF], axis=0, keepdims=True)
        hood.append(jnp.concatenate([part.astype(BF16) for part in (fine, *pair)], axis=0))
        vectors.append(values[KF:].astype(BF16))
    gram = jnp.dot(edges, jnp.concatenate(hood, axis=1), preferred_element_type=F32)
    added = lax.dot_general(
        jnp.concatenate(vectors, axis=1),
        (taper * gram).astype(BF16),
        (((1,), (1,)), ((), ())),
        preferred_element_type=F32,
    )
    outer = (slot == 0) | (slot == 7)
    return [
        jnp.where(outer, pltpu.roll(added, (7 - 2 * a) * LAT_REACH, 1), 0.0) for a in range(CLON)
    ]


def core_kernel(
    parity, weights, off_chip, own, early, late, near, out, edges, far_taper, hood, mine, vectors, taper
):
    tiles = Hood(parity, off_chip, own, early, late)
    i = lax.broadcasted_iota(jnp.int32, (CLAT, CLAT), 0)
    j = lax.broadcasted_iota(jnp.int32, (CLAT, CLAT), 1)
    gap = jnp.abs(i - j)
    ratio = gap.astype(F32) * (1.0 / LAT_REACH)
    band = jnp.where(gap <= LAT_REACH, 1.0 - 0.75 * ratio * ratio, 0.0)
    for distance in range(LON_REACH + 1):
        taper[distance] = band * lon_weight(distance)
    level = weights[...]
    weight_fine = level[:, :1] * (1.0 / (KF - 1))
    weight_coarse = level[:, 1:] * (1.0 / (KC - 1))
    weight_paired = level[:, 1:] * (-1.0 / (KF - 1))
    lane = lax.broadcasted_iota(jnp.int32, (1, CLAT), 1) // LAT_REACH
    both = jnp.zeros((KX, CLAT), F32)
    coarse_columns = [tiles.coarse(m).astype(F32) for m in range(6)]
    for b in COLUMNS:
        block = tiles.fv(b)
        refined = coarse_columns[b // 2]
        if b % 2:
            refined = 0.5 * (refined + coarse_columns[b // 2 + 1])
        fine, coarse, paired = anomaly_rows(block[:KF].astype(F32), refined)
        lanes = slice((b - 1) * CLAT, b * CLAT)
        hood[:KF, lanes] = fine.astype(BF16)
        hood[KF : KF + KC, lanes] = coarse.astype(BF16)
        hood[KF + KC :, lanes] = paired.astype(BF16)
        vectors[:, lanes] = block[KF:]
        if CLON <= b < 2 * CLON:
            a = b - CLON
            scaled = jnp.concatenate(
                (weight_fine * fine, weight_coarse * coarse, weight_paired * paired), axis=0
            )
            mine[:, a * CLAT : (a + 1) * CLAT] = scaled.astype(BF16)
            moved = pltpu.roll(scaled, (2 * a + 1) * LAT_REACH, 1)
            both = jnp.where(lane // 2 == a, moved, both)
    edges[...] = both.T.astype(BF16)
    odd = lax.axis_index("lat") % 2 == 1
    far_taper[...] = jnp.concatenate([rim_taper(odd, n) for n in range(2)], axis=1)
    near_taper = jnp.concatenate([rim_taper(~odd, n) for n in range(2)], axis=1)
    near_terms = rim_terms(near[...], edges[...], near_taper, ~odd)
    for a in range(CLON):
        lanes = slice(a * CLAT, (a + 7) * CLAT)
        gram = lax.dot_general(
            mine[:, a * CLAT : (a + 1) * CLAT],
            hood[:, lanes],
            (((0,), (0,)), ((), ())),
            preferred_element_type=F32,
        )
        tapered = jnp.concatenate(
            [
                (taper[abs(n - LON_REACH)] * gram[:, n * CLAT : (n + 1) * CLAT]).astype(BF16)
                for n in range(7)
            ],
            axis=1,
        )
        out[a] = near_terms[a] + lax.dot_general(
            vectors[:, lanes], tapered, (((1,), (1,)), ((), ())), preferred_element_type=F32
        )


def rim_kernel(parity, core, edges, far_taper, far, out):
    odd = lax.axis_index("lat") % 2 == 1
    terms = rim_terms(far[...], edges[...], far_taper[...], odd)
    for a in range(CLON):
        out[pl.ds(a, NV, stride=CLON), :] = core[a] + terms[a]


def last_kernel(even_out, core, edges, far_taper, far, out):
    odd = lax.axis_index("lon") % 2 == 1

    @pl.when(odd)
    def _():
        rim_kernel(1, core, edges, far_taper, far, out)

    @pl.when(~odd)
    def _():
        out[...] = even_out[...]


def call(kernel, outs, in_specs, scratch, flops, moved):
    return pl.pallas_call(
        kernel,
        out_shape=[jax.ShapeDtypeStruct(shape, dtype) for shape, dtype in outs],
        in_specs=in_specs,
        out_specs=[VMEM] * len(outs),
        scratch_shapes=scratch,
        compiler_params=pltpu.CompilerParams(vmem_limit_bytes=24 << 20),
        cost_estimate=pl.CostEstimate(flops=flops, bytes_accessed=moved, transcendentals=0),
    )


def in_hbm(array):
    return pltpu.with_memory_space_constraint(array, pltpu.HBM)


def partner(k, first):
    return ((k - first) ^ 1) + first


def swap_lat(block, first, parity):
    lon, lat = lax.axis_size("lon"), lax.axis_size("lat")
    pairs = [(k, partner(k, first)) for k in range(lat) if 0 <= partner(k, first) < lat]
    pairs = [(n * lat + k, n * lat + to) for n in range(parity, lon, 2) for k, to in pairs]
    return lax.ppermute(block, ("lon", "lat"), pairs)


def send_lon(block, first, chosen):
    n = lax.axis_size("lon")
    return lax.ppermute(block, "lon", [(k, partner(k, first) % n) for k in range(n) if chosen(k)])


def per_device(fine_members, coarse_members, increments, level_weights):
    shapes = ((128, CLAT), (256, CLAT), (128, CLAT))
    own, to_east, early, on_chip = call(
        pack_kernel,
        [((rows, CLAT), BF16) for rows in (PADDED, EASTWARD, EARLY, SENT)],
        [pl.BlockSpec(memory_space=pltpu.HBM)] * 3,
        [pltpu.VMEM(shape, BF16) for shape in shapes]
        + [pltpu.VMEM(shape, F32) for shape in shapes]
        + [pltpu.SemaphoreType.DMA((4,))],
        1 << 20,
        1 << 19,
    )(
        in_hbm(fine_members.reshape(KF * CLON, CLAT)),
        in_hbm(coarse_members.reshape(KC * 2, CLAT)),
        in_hbm(increments.reshape(NV * CLON, CLAT)),
    )
    from_west = send_lon(to_east, 1, lambda k: k % 2 == 1)
    early = send_lon(early, 0, lambda k: k % RING < 2)
    from_east = send_lon(own, 1, lambda k: k % 2 == 0)
    late = send_lon(on_chip, 0, lambda k: k % RING >= 2)
    cores, after = [], own
    for parity, received in ((0, from_west), (1, from_east)):
        near, far = call(
            for_parity(parity, edge_kernel),
            [((EDGE, CLAT), BF16), ((EDGE, CLAT), BF16)],
            [VMEM] * 5,
            [],
            1,
            1,
        )(received, own, early, late, after)
        after = near
        near = swap_lat(near, 0, parity)
        far = swap_lat(far, 1, parity)
        core = call(
            for_parity(parity, core_kernel),
            [
                ((CLON, NV, CLAT), F32),
                ((CLAT, KX), BF16),
                ((CLAT, 2 * CLAT), F32),
            ],
            [VMEM] * 6,
            [
                pltpu.VMEM((KX, 10 * CLAT), BF16),
                pltpu.VMEM((KX, CLON * CLAT), BF16),
                pltpu.VMEM((NV, 10 * CLAT), BF16),
                pltpu.VMEM((LON_REACH + 1, CLAT, CLAT), F32),
            ],
            200 << 20,
            4 << 20,
        )(level_weights.reshape(1, 2), received, own, early, late, near)
        cores.append((*core, far))
    result = ((NV * CLON, CLAT), F32)
    (even_out,) = call(for_parity(0, rim_kernel), [result], [VMEM] * 4, [], 8 << 20, 1 << 19)(*cores[0])
    (out,) = call(last_kernel, [result], [VMEM] * 5, [], 8 << 20, 1 << 19)(even_out, *cores[1])
    return out.reshape(NV, CLON, CLAT)


def solution(mesh):
    in_specs = (P(None, "lon", "lat"), P(None, "lon", "lat"), P(None, "lon", "lat"), P())
    out_specs = P(None, "lon", "lat")
    return jax.shard_map(
        per_device, mesh=mesh, in_specs=in_specs, out_specs=out_specs, check_vma=False
    )
```

```python
import jax
import jax.numpy as jnp
from jax import lax
from jax.experimental import pallas as pl
from jax.experimental.pallas import tpu as pltpu
from jax.sharding import PartitionSpec as P

KF, KC, NV = 32, 128, 32
CLON, CLAT = 4, 128
LON_REACH, LAT_REACH = 3, 16
FV = KF + NV
KX = KF + KC + KF
SENT = 3 * FV + 2 * KC
TILE = 4 * FV + 2 * KC
PADDED, EASTWARD, EARLY = 536, 472, 464
EDGE = KC + FV
COLUMNS = range(1, 11)
RING = 16
VMEM = pl.BlockSpec(memory_space=pltpu.VMEM)
F32, BF16 = jnp.float32, jnp.bfloat16

OWN_FV = (0, 64, 128, 448)
OWN_C = (192, 320)
WEST_FV = (None, 0, 64, 384)
WEST_C = (128, 256)
EAST_FV = (0, 64, 128, None)
EAST_C = (192, 320)


def lon_weight(distance):
    return 1.0 - 0.75 * (distance / LON_REACH) ** 2


class Hood:
    def __init__(self, parity, off_chip, own, early, late):
        self.parity, self.off_chip, self.own, self.early, self.late = parity, off_chip, own, early, late
        self.is_early = lax.axis_index("lon") % RING < 2

    def rows(self, tile, at, count):
        if tile == 1:
            return self.own[at : at + count, :]
        if (tile == 0) == (self.parity == 0):
            return self.off_chip[at : at + count, :]
        early, late = self.early[at : at + count, :], self.late[at : at + count, :]
        return jnp.where(self.is_early, early, late)

    def fv(self, column):
        tile, at = divmod(column, CLON)
        return self.rows(tile, (WEST_FV, OWN_FV, EAST_FV)[tile][at], FV)

    def coarse(self, column):
        tile, at = divmod(column, 2)
        return self.rows(tile, (WEST_C, OWN_C, EAST_C)[tile][at], KC)


def pack_kernel(
    fine, coarse, vectors, own, to_east, early, on_chip, fine16, coarse16, vectors16, fine32, coarse32, vectors32, sem
):
    half = KC
    pairs = (
        (fine, fine16),
        (coarse.at[:half], coarse16.at[:half]),
        (coarse.at[half:], coarse16.at[half:]),
        (vectors, vectors16),
    )
    copies = [pltpu.make_async_copy(src, dst, sem.at[n]) for n, (src, dst) in enumerate(pairs)]
    for n in (1, 2, 0, 3):
        copies[n].start()
    odd = lax.axis_index("lon") % 2 == 1

    def put(block, at):
        own[at : at + block.shape[0], :] = block

    copies[0].wait()
    fine32[...] = fine16[...].astype(F32)
    for a in range(CLON):
        put(fine32[pl.ds(a, KF, stride=CLON), :].astype(BF16), OWN_FV[a])
    copies[3].wait()
    vectors32[...] = vectors16[...].astype(F32)
    for a in range(CLON):
        put(vectors32[pl.ds(a, NV, stride=CLON), :].astype(BF16), OWN_FV[a] + KF)
    copies[1].wait()
    copies[2].wait()
    coarse32[...] = coarse16[...].astype(F32)
    for m in range(2):
        put(coarse32[pl.ds(m, KC, stride=2), :].astype(BF16), OWN_C[m])
    own[TILE:, :] = jnp.zeros((PADDED - TILE, CLAT), BF16)
    to_east[:SENT, :] = own[FV:TILE, :]
    to_east[SENT:, :] = jnp.zeros((EASTWARD - SENT, CLAT), BF16)
    trimmed = jnp.where(odd, own[:SENT, :], own[FV:TILE, :])
    early[:SENT, :] = trimmed
    early[SENT:, :] = jnp.zeros((EARLY - SENT, CLAT), BF16)
    on_chip[...] = trimmed


def for_parity(parity, body):
    def kernel(*refs):
        @pl.when(lax.axis_index("lon") % 2 == parity)
        def _():
            body(parity, *refs)

    return kernel


def edge_kernel(parity, off_chip, own, early, late, after, near, far):
    hood = Hood(parity, off_chip, own, early, late)
    odd = lax.axis_index("lat") % 2 == 1
    lane = lax.broadcasted_iota(jnp.int32, (1, CLAT), 1) // LAT_REACH

    def gather(blocks, at):
        high = jnp.zeros((FV, CLAT), F32)
        low = jnp.zeros((FV, CLAT), F32)
        for slot, block in blocks.items():
            shift = (slot + 1) % 8 * LAT_REACH
            block = block.astype(F32)
            moved = pltpu.roll(block, shift, 1) if shift else block
            high = jnp.where(lane == slot, moved, high)
            low = jnp.where(lane == (slot + 1) % 8, moved, low)
        near[at : at + FV, :] = jnp.where(odd, low, high).astype(BF16)
        far[at : at + FV, :] = jnp.where(odd, high, low).astype(BF16)

    even = {m: hood.fv(2 * m) for m in range(1, 6)}
    uneven = {m: hood.fv(2 * m + 1) for m in range(0, 5)}
    coarse = {m: hood.coarse(m) for m in range(6)}
    upper = {m: block[:FV] for m, block in coarse.items()}
    upper.update({6: even[3], 7: even[4]})
    gather(upper, 0)
    gather({m: block[FV:] for m, block in coarse.items()}, FV)
    gather({**uneven, 5: even[5], 6: even[1], 7: even[2]}, KC)


def anomaly_rows(fine, refined):
    fine = fine - jnp.mean(fine, axis=0, keepdims=True)
    coarse = refined - jnp.mean(refined, axis=0, keepdims=True)
    paired = refined[:KF]
    paired = paired - jnp.mean(paired, axis=0, keepdims=True)
    return fine, coarse, paired


def rim_taper(is_above, parity):
    above = is_above.astype(jnp.int32)
    row = lax.broadcasted_iota(jnp.int32, (CLAT, CLAT), 0)
    lane = lax.broadcasted_iota(jnp.int32, (CLAT, CLAT), 1)
    column = 2 * (lane // LAT_REACH - above) + parity
    lon_gap = jnp.abs(column - CLON - row // (2 * LAT_REACH))
    shift = lane % LAT_REACH - row % LAT_REACH
    lat_gap = LAT_REACH + (2 * above - 1) * shift
    lon_ratio = lon_gap.astype(F32) * (1.0 / LON_REACH)
    lat_ratio = lat_gap.astype(F32) * (1.0 / LAT_REACH)
    here = row // LAT_REACH % 2 + above == 1
    inside = here & (lon_gap <= LON_REACH) & (lat_gap <= LAT_REACH)
    value = (1.0 - 0.75 * lon_ratio * lon_ratio) * (1.0 - 0.75 * lat_ratio * lat_ratio)
    return jnp.where(inside, value, 0.0)


def halfway(values):
    return 0.5 * (values + pltpu.roll(values, CLAT - LAT_REACH, 1))


def rim_terms(rim, edges, taper, is_above):
    refined = rim[:KC].astype(F32)
    coarse = refined - jnp.mean(refined, axis=0, keepdims=True)
    paired = refined[:KF] - jnp.mean(refined[:KF], axis=0, keepdims=True)
    slot = lax.broadcasted_iota(jnp.int32, (1, CLAT), 1) // LAT_REACH
    own_slot = (slot + 8 - is_above.astype(jnp.int32)) % 8
    mixed = rim[KC:].astype(F32)
    even = jnp.where(own_slot <= 2, pltpu.roll(mixed, 3 * LAT_REACH, 1), pltpu.roll(refined[:FV], 5 * LAT_REACH, 1))
    even = jnp.where(own_slot >= 5, mixed, even)
    hood, vectors = [], []
    for values, pair in ((even, (coarse, paired)), (mixed, (halfway(coarse), halfway(paired)))):
        fine = values[:KF] - jnp.mean(values[:KF], axis=0, keepdims=True)
        hood.append(jnp.concatenate([part.astype(BF16) for part in (fine, *pair)], axis=0))
        vectors.append(values[KF:].astype(BF16))
    gram = jnp.dot(edges, jnp.concatenate(hood, axis=1), preferred_element_type=F32)
    added = lax.dot_general(
        jnp.concatenate(vectors, axis=1),
        (taper * gram).astype(BF16),
        (((1,), (1,)), ((), ())),
        preferred_element_type=F32,
    )
    outer = (slot == 0) | (slot == 7)
    return [
        jnp.where(outer, pltpu.roll(added, (7 - 2 * a) * LAT_REACH, 1), 0.0) for a in range(CLON)
    ]


def core_kernel(
    parity, weights, off_chip, own, early, late, near, out, edges, far_taper, hood, mine, vectors, taper
):
    tiles = Hood(parity, off_chip, own, early, late)
    i = lax.broadcasted_iota(jnp.int32, (CLAT, CLAT), 0)
    j = lax.broadcasted_iota(jnp.int32, (CLAT, CLAT), 1)
    gap = jnp.abs(i - j)
    ratio = gap.astype(F32) * (1.0 / LAT_REACH)
    band = jnp.where(gap <= LAT_REACH, 1.0 - 0.75 * ratio * ratio, 0.0)
    for distance in range(LON_REACH + 1):
        taper[distance] = band * lon_weight(distance)
    level = weights[...]
    weight_fine = level[:, :1] * (1.0 / (KF - 1))
    weight_coarse = level[:, 1:] * (1.0 / (KC - 1))
    weight_paired = level[:, 1:] * (-1.0 / (KF - 1))
    lane = lax.broadcasted_iota(jnp.int32, (1, CLAT), 1) // LAT_REACH
    both = jnp.zeros((KX, CLAT), F32)
    coarse_columns = [tiles.coarse(m).astype(F32) for m in range(6)]
    for b in COLUMNS:
        block = tiles.fv(b)
        refined = coarse_columns[b // 2]
        if b % 2:
            refined = 0.5 * (refined + coarse_columns[b // 2 + 1])
        fine, coarse, paired = anomaly_rows(block[:KF].astype(F32), refined)
        lanes = slice((b - 1) * CLAT, b * CLAT)
        hood[:KF, lanes] = fine.astype(BF16)
        hood[KF : KF + KC, lanes] = coarse.astype(BF16)
        hood[KF + KC :, lanes] = paired.astype(BF16)
        vectors[:, lanes] = block[KF:]
        if CLON <= b < 2 * CLON:
            a = b - CLON
            scaled = jnp.concatenate(
                (weight_fine * fine, weight_coarse * coarse, weight_paired * paired), axis=0
            )
            mine[:, a * CLAT : (a + 1) * CLAT] = scaled.astype(BF16)
            moved = pltpu.roll(scaled, (2 * a + 1) * LAT_REACH, 1)
            both = jnp.where(lane // 2 == a, moved, both)
    edges[...] = both.T.astype(BF16)
    odd = lax.axis_index("lat") % 2 == 1
    far_taper[...] = jnp.concatenate([rim_taper(odd, n) for n in range(2)], axis=1)
    near_taper = jnp.concatenate([rim_taper(~odd, n) for n in range(2)], axis=1)
    near_terms = rim_terms(near[...], edges[...], near_taper, ~odd)
    for a in range(CLON):
        lanes = slice(a * CLAT, (a + 7) * CLAT)
        gram = lax.dot_general(
            mine[:, a * CLAT : (a + 1) * CLAT],
            hood[:, lanes],
            (((0,), (0,)), ((), ())),
            preferred_element_type=F32,
        )
        tapered = jnp.concatenate(
            [
                (taper[abs(n - LON_REACH)] * gram[:, n * CLAT : (n + 1) * CLAT]).astype(BF16)
                for n in range(7)
            ],
            axis=1,
        )
        out[a] = near_terms[a] + lax.dot_general(
            vectors[:, lanes], tapered, (((1,), (1,)), ((), ())), preferred_element_type=F32
        )


def rim_kernel(parity, core, edges, far_taper, far, out):
    odd = lax.axis_index("lat") % 2 == 1
    terms = rim_terms(far[...], edges[...], far_taper[...], odd)
    for a in range(CLON):
        out[pl.ds(a, NV, stride=CLON), :] = core[a] + terms[a]


def last_kernel(even_out, core, edges, far_taper, far, out):
    odd = lax.axis_index("lon") % 2 == 1

    @pl.when(odd)
    def _():
        rim_kernel(1, core, edges, far_taper, far, out)

    @pl.when(~odd)
    def _():
        out[...] = even_out[...]


def call(kernel, outs, in_specs, scratch, flops, moved):
    return pl.pallas_call(
        kernel,
        out_shape=[jax.ShapeDtypeStruct(shape, dtype) for shape, dtype in outs],
        in_specs=in_specs,
        out_specs=[VMEM] * len(outs),
        scratch_shapes=scratch,
        compiler_params=pltpu.CompilerParams(vmem_limit_bytes=24 << 20),
        cost_estimate=pl.CostEstimate(flops=flops, bytes_accessed=moved, transcendentals=0),
    )


def in_hbm(array):
    return pltpu.with_memory_space_constraint(array, pltpu.HBM)


def partner(k, first):
    return ((k - first) ^ 1) + first


def swap_lat(block, first, parity):
    lon, lat = lax.axis_size("lon"), lax.axis_size("lat")
    pairs = [(k, partner(k, first)) for k in range(lat) if 0 <= partner(k, first) < lat]
    pairs = [(n * lat + k, n * lat + to) for n in range(parity, lon, 2) for k, to in pairs]
    return lax.ppermute(block, ("lon", "lat"), pairs)


def send_lon(block, first, chosen):
    n = lax.axis_size("lon")
    return lax.ppermute(block, "lon", [(k, partner(k, first) % n) for k in range(n) if chosen(k)])


def per_device(fine_members, coarse_members, increments, level_weights):
    shapes = ((128, CLAT), (256, CLAT), (128, CLAT))
    own, to_east, early, on_chip = call(
        pack_kernel,
        [((rows, CLAT), BF16) for rows in (PADDED, EASTWARD, EARLY, SENT)],
        [pl.BlockSpec(memory_space=pltpu.HBM)] * 3,
        [pltpu.VMEM(shape, BF16) for shape in shapes]
        + [pltpu.VMEM(shape, F32) for shape in shapes]
        + [pltpu.SemaphoreType.DMA((4,))],
        1 << 20,
        1 << 19,
    )(
        in_hbm(fine_members.reshape(KF * CLON, CLAT)),
        in_hbm(coarse_members.reshape(KC * 2, CLAT)),
        in_hbm(increments.reshape(NV * CLON, CLAT)),
    )
    from_west = send_lon(to_east, 1, lambda k: k % 2 == 1)
    early = send_lon(early, 0, lambda k: k % RING < 2)
    from_east = send_lon(own, 1, lambda k: k % 2 == 0)
    late = send_lon(on_chip, 0, lambda k: k % RING >= 2)
    cores, after = [], own
    for parity, received in ((0, from_west), (1, from_east)):
        near, far = call(
            for_parity(parity, edge_kernel),
            [((EDGE, CLAT), BF16), ((EDGE, CLAT), BF16)],
            [VMEM] * 5,
            [],
            1,
            1,
        )(received, own, early, late, after)
        after = near
        near = swap_lat(near, 0, parity)
        far = swap_lat(far, 1, parity)
        core = call(
            for_parity(parity, core_kernel),
            [
                ((CLON, NV, CLAT), F32),
                ((CLAT, KX), BF16),
                ((CLAT, 2 * CLAT), F32),
            ],
            [VMEM] * 6,
            [
                pltpu.VMEM((KX, 10 * CLAT), BF16),
                pltpu.VMEM((KX, CLON * CLAT), BF16),
                pltpu.VMEM((NV, 10 * CLAT), BF16),
                pltpu.VMEM((LON_REACH + 1, CLAT, CLAT), F32),
            ],
            200 << 20,
            4 << 20,
        )(level_weights.reshape(1, 2), received, own, early, late, near)
        cores.append((*core, far))
    result = ((NV * CLON, CLAT), F32)
    (even_out,) = call(for_parity(0, rim_kernel), [result], [VMEM] * 4, [], 8 << 20, 1 << 19)(*cores[0])
    (out,) = call(last_kernel, [result], [VMEM] * 5, [], 8 << 20, 1 << 19)(even_out, *cores[1])
    return out.reshape(NV, CLON, CLAT)


def solution(mesh):
    in_specs = (P(None, "lon", "lat"), P(None, "lon", "lat"), P(None, "lon", "lat"), P())
    out_specs = P(None, "lon", "lat")
    return jax.shard_map(
        per_device, mesh=mesh, in_specs=in_specs, out_specs=out_specs, check_vma=False
    )
```

```python
import jax
import jax.numpy as jnp
from jax import lax
from jax.experimental import pallas as pl
from jax.experimental.pallas import tpu as pltpu
from jax.sharding import PartitionSpec as P

KF, KC, NV = 32, 128, 32
CLON, CLAT = 4, 128
LON_REACH, LAT_REACH = 3, 16
FV = KF + NV
KX = KF + KC + KF
SENT = 3 * FV + 2 * KC
TILE = 4 * FV + 2 * KC
PADDED, EASTWARD, EARLY = 536, 472, 464
EDGE = KC + FV
COLUMNS = range(1, 11)
RING = 16
VMEM = pl.BlockSpec(memory_space=pltpu.VMEM)
F32, BF16 = jnp.float32, jnp.bfloat16

OWN_FV = (0, 64, 128, 448)
OWN_C = (192, 320)
WEST_FV = (None, 0, 64, 384)
WEST_C = (128, 256)
EAST_FV = (0, 64, 128, None)
EAST_C = (192, 320)


def lon_weight(distance):
    return 1.0 - 0.75 * (distance / LON_REACH) ** 2


class Hood:
    def __init__(self, parity, off_chip, own, early, late):
        self.parity, self.off_chip, self.own, self.early, self.late = parity, off_chip, own, early, late
        self.is_early = lax.axis_index("lon") % RING < 2

    def rows(self, tile, at, count):
        if tile == 1:
            return self.own[at : at + count, :]
        if (tile == 0) == (self.parity == 0):
            return self.off_chip[at : at + count, :]
        early, late = self.early[at : at + count, :], self.late[at : at + count, :]
        return jnp.where(self.is_early, early, late)

    def fv(self, column):
        tile, at = divmod(column, CLON)
        return self.rows(tile, (WEST_FV, OWN_FV, EAST_FV)[tile][at], FV)

    def coarse(self, column):
        tile, at = divmod(column, 2)
        return self.rows(tile, (WEST_C, OWN_C, EAST_C)[tile][at], KC)


def pack_kernel(
    fine, coarse, vectors, own, to_east, early, on_chip, fine16, coarse16, vectors16, fine32, coarse32, vectors32, sem
):
    half = KC
    pairs = (
        (fine, fine16),
        (coarse.at[:half], coarse16.at[:half]),
        (coarse.at[half:], coarse16.at[half:]),
        (vectors, vectors16),
    )
    copies = [pltpu.make_async_copy(src, dst, sem.at[n]) for n, (src, dst) in enumerate(pairs)]
    for copy in copies:
        copy.start()
    odd = lax.axis_index("lon") % 2 == 1

    def put(block, at):
        own[at : at + block.shape[0], :] = block

    copies[0].wait()
    fine32[...] = fine16[...].astype(F32)
    for a in range(CLON):
        put(fine32[pl.ds(a, KF, stride=CLON), :].astype(BF16), OWN_FV[a])
    copies[1].wait()
    copies[2].wait()
    coarse32[...] = coarse16[...].astype(F32)
    for m in range(2):
        put(coarse32[pl.ds(m, KC, stride=2), :].astype(BF16), OWN_C[m])
    copies[3].wait()
    vectors32[...] = vectors16[...].astype(F32)
    for a in range(CLON):
        put(vectors32[pl.ds(a, NV, stride=CLON), :].astype(BF16), OWN_FV[a] + KF)
    own[TILE:, :] = jnp.zeros((PADDED - TILE, CLAT), BF16)
    to_east[:SENT, :] = own[FV:TILE, :]
    to_east[SENT:, :] = jnp.zeros((EASTWARD - SENT, CLAT), BF16)
    trimmed = jnp.where(odd, own[:SENT, :], own[FV:TILE, :])
    early[:SENT, :] = trimmed
    early[SENT:, :] = jnp.zeros((EARLY - SENT, CLAT), BF16)
    on_chip[...] = trimmed


def for_parity(parity, body):
    def kernel(*refs):
        @pl.when(lax.axis_index("lon") % 2 == parity)
        def _():
            body(parity, *refs)

    return kernel


def edge_kernel(parity, off_chip, own, early, late, after, near, far):
    hood = Hood(parity, off_chip, own, early, late)
    odd = lax.axis_index("lat") % 2 == 1
    lane = lax.broadcasted_iota(jnp.int32, (1, CLAT), 1) // LAT_REACH

    def gather(blocks, at):
        high = jnp.zeros((FV, CLAT), BF16)
        low = jnp.zeros((FV, CLAT), BF16)
        for slot, block in blocks.items():
            shift = (slot + 1) % 8 * LAT_REACH
            moved = pltpu.roll(block, shift, 1) if shift else block
            high = jnp.where(lane == slot, moved, high)
            low = jnp.where(lane == (slot + 1) % 8, moved, low)
        near[at : at + FV, :] = jnp.where(odd, low, high)
        far[at : at + FV, :] = jnp.where(odd, high, low)

    even = {m: hood.fv(2 * m) for m in range(1, 6)}
    uneven = {m: hood.fv(2 * m + 1) for m in range(0, 5)}
    coarse = {m: hood.coarse(m) for m in range(6)}
    upper = {m: block[:FV] for m, block in coarse.items()}
    upper.update({6: even[3], 7: even[4]})
    gather(upper, 0)
    gather({m: block[FV:] for m, block in coarse.items()}, FV)
    gather({**uneven, 5: even[5], 6: even[1], 7: even[2]}, KC)


def anomaly_rows(fine, refined):
    fine = fine - jnp.mean(fine, axis=0, keepdims=True)
    coarse = refined - jnp.mean(refined, axis=0, keepdims=True)
    paired = refined[:KF]
    paired = paired - jnp.mean(paired, axis=0, keepdims=True)
    return fine, coarse, paired


def rim_taper(is_above, parity):
    above = is_above.astype(jnp.int32)
    row = lax.broadcasted_iota(jnp.int32, (CLAT, CLAT), 0)
    lane = lax.broadcasted_iota(jnp.int32, (CLAT, CLAT), 1)
    column = 2 * (lane // LAT_REACH - above) + parity
    lon_gap = jnp.abs(column - CLON - row // (2 * LAT_REACH))
    shift = lane % LAT_REACH - row % LAT_REACH
    lat_gap = LAT_REACH + (2 * above - 1) * shift
    lon_ratio = lon_gap.astype(F32) * (1.0 / LON_REACH)
    lat_ratio = lat_gap.astype(F32) * (1.0 / LAT_REACH)
    here = row // LAT_REACH % 2 + above == 1
    inside = here & (lon_gap <= LON_REACH) & (lat_gap <= LAT_REACH)
    value = (1.0 - 0.75 * lon_ratio * lon_ratio) * (1.0 - 0.75 * lat_ratio * lat_ratio)
    return jnp.where(inside, value, 0.0)


def halfway(values):
    return 0.5 * (values + pltpu.roll(values, CLAT - LAT_REACH, 1))


def rim_terms(rim, edges, taper, is_above):
    refined = rim[:KC].astype(F32)
    coarse = refined - jnp.mean(refined, axis=0, keepdims=True)
    paired = refined[:KF] - jnp.mean(refined[:KF], axis=0, keepdims=True)
    slot = lax.broadcasted_iota(jnp.int32, (1, CLAT), 1) // LAT_REACH
    own_slot = (slot + 8 - is_above.astype(jnp.int32)) % 8
    mixed = rim[KC:].astype(F32)
    even = jnp.where(own_slot <= 2, pltpu.roll(mixed, 3 * LAT_REACH, 1), pltpu.roll(refined[:FV], 5 * LAT_REACH, 1))
    even = jnp.where(own_slot >= 5, mixed, even)
    hood, vectors = [], []
    for values, pair in ((even, (coarse, paired)), (mixed, (halfway(coarse), halfway(paired)))):
        fine = values[:KF] - jnp.mean(values[:KF], axis=0, keepdims=True)
        hood.append(jnp.concatenate([part.astype(BF16) for part in (fine, *pair)], axis=0))
        vectors.append(values[KF:].astype(BF16))
    gram = jnp.dot(edges, jnp.concatenate(hood, axis=1), preferred_element_type=F32)
    added = lax.dot_general(
        jnp.concatenate(vectors, axis=1),
        (taper * gram).astype(BF16),
        (((1,), (1,)), ((), ())),
        preferred_element_type=F32,
    )
    outer = (slot == 0) | (slot == 7)
    return [
        jnp.where(outer, pltpu.roll(added, (7 - 2 * a) * LAT_REACH, 1), 0.0) for a in range(CLON)
    ]


def core_kernel(
    parity, weights, off_chip, own, early, late, near, out, edges, far_taper, hood, mine, vectors, taper
):
    tiles = Hood(parity, off_chip, own, early, late)
    i = lax.broadcasted_iota(jnp.int32, (CLAT, CLAT), 0)
    j = lax.broadcasted_iota(jnp.int32, (CLAT, CLAT), 1)
    gap = jnp.abs(i - j)
    ratio = gap.astype(F32) * (1.0 / LAT_REACH)
    band = jnp.where(gap <= LAT_REACH, 1.0 - 0.75 * ratio * ratio, 0.0)
    for distance in range(LON_REACH + 1):
        taper[distance] = band * lon_weight(distance)
    level = weights[...]
    weight_fine = level[:, :1] * (1.0 / (KF - 1))
    weight_coarse = level[:, 1:] * (1.0 / (KC - 1))
    weight_paired = level[:, 1:] * (-1.0 / (KF - 1))
    lane = lax.broadcasted_iota(jnp.int32, (1, CLAT), 1) // LAT_REACH
    both = jnp.zeros((KX, CLAT), F32)
    coarse_columns = [tiles.coarse(m).astype(F32) for m in range(6)]
    for b in COLUMNS:
        block = tiles.fv(b)
        refined = coarse_columns[b // 2]
        if b % 2:
            refined = 0.5 * (refined + coarse_columns[b // 2 + 1])
        fine, coarse, paired = anomaly_rows(block[:KF].astype(F32), refined)
        lanes = slice((b - 1) * CLAT, b * CLAT)
        hood[:KF, lanes] = fine.astype(BF16)
        hood[KF : KF + KC, lanes] = coarse.astype(BF16)
        hood[KF + KC :, lanes] = paired.astype(BF16)
        vectors[:, lanes] = block[KF:]
        if CLON <= b < 2 * CLON:
            a = b - CLON
            scaled = jnp.concatenate(
                (weight_fine * fine, weight_coarse * coarse, weight_paired * paired), axis=0
            )
            mine[:, a * CLAT : (a + 1) * CLAT] = scaled.astype(BF16)
            moved = pltpu.roll(scaled, (2 * a + 1) * LAT_REACH, 1)
            both = jnp.where(lane // 2 == a, moved, both)
    edges[...] = both.T.astype(BF16)
    odd = lax.axis_index("lat") % 2 == 1
    far_taper[...] = jnp.concatenate([rim_taper(odd, n) for n in range(2)], axis=1)
    near_taper = jnp.concatenate([rim_taper(~odd, n) for n in range(2)], axis=1)
    near_terms = rim_terms(near[...], edges[...], near_taper, ~odd)
    for a in range(CLON):
        lanes = slice(a * CLAT, (a + 7) * CLAT)
        gram = lax.dot_general(
            mine[:, a * CLAT : (a + 1) * CLAT],
            hood[:, lanes],
            (((0,), (0,)), ((), ())),
            preferred_element_type=F32,
        )
        tapered = jnp.concatenate(
            [
                (taper[abs(n - LON_REACH)] * gram[:, n * CLAT : (n + 1) * CLAT]).astype(BF16)
                for n in range(7)
            ],
            axis=1,
        )
        out[a] = near_terms[a] + lax.dot_general(
            vectors[:, lanes], tapered, (((1,), (1,)), ((), ())), preferred_element_type=F32
        )


def rim_kernel(parity, core, edges, far_taper, far, out):
    odd = lax.axis_index("lat") % 2 == 1
    terms = rim_terms(far[...], edges[...], far_taper[...], odd)
    for a in range(CLON):
        out[pl.ds(a, NV, stride=CLON), :] = core[a] + terms[a]


def last_kernel(even_out, core, edges, far_taper, far, out):
    odd = lax.axis_index("lon") % 2 == 1

    @pl.when(odd)
    def _():
        rim_kernel(1, core, edges, far_taper, far, out)

    @pl.when(~odd)
    def _():
        out[...] = even_out[...]


def call(kernel, outs, in_specs, scratch, flops, moved):
    return pl.pallas_call(
        kernel,
        out_shape=[jax.ShapeDtypeStruct(shape, dtype) for shape, dtype in outs],
        in_specs=in_specs,
        out_specs=[VMEM] * len(outs),
        scratch_shapes=scratch,
        compiler_params=pltpu.CompilerParams(vmem_limit_bytes=24 << 20),
        cost_estimate=pl.CostEstimate(flops=flops, bytes_accessed=moved, transcendentals=0),
    )


def in_hbm(array):
    return pltpu.with_memory_space_constraint(array, pltpu.HBM)


def partner(k, first):
    return ((k - first) ^ 1) + first


def swap_lat(block, first, parity):
    lon, lat = lax.axis_size("lon"), lax.axis_size("lat")
    pairs = [(k, partner(k, first)) for k in range(lat) if 0 <= partner(k, first) < lat]
    pairs = [(n * lat + k, n * lat + to) for n in range(parity, lon, 2) for k, to in pairs]
    return lax.ppermute(block, ("lon", "lat"), pairs)


def send_lon(block, first, chosen):
    n = lax.axis_size("lon")
    return lax.ppermute(block, "lon", [(k, partner(k, first) % n) for k in range(n) if chosen(k)])


def per_device(fine_members, coarse_members, increments, level_weights):
    shapes = ((128, CLAT), (256, CLAT), (128, CLAT))
    own, to_east, early, on_chip = call(
        pack_kernel,
        [((rows, CLAT), BF16) for rows in (PADDED, EASTWARD, EARLY, SENT)],
        [pl.BlockSpec(memory_space=pltpu.HBM)] * 3,
        [pltpu.VMEM(shape, BF16) for shape in shapes]
        + [pltpu.VMEM(shape, F32) for shape in shapes]
        + [pltpu.SemaphoreType.DMA((4,))],
        1 << 20,
        1 << 19,
    )(
        in_hbm(fine_members.reshape(KF * CLON, CLAT)),
        in_hbm(coarse_members.reshape(KC * 2, CLAT)),
        in_hbm(increments.reshape(NV * CLON, CLAT)),
    )
    from_west = send_lon(to_east, 1, lambda k: k % 2 == 1)
    early = send_lon(early, 0, lambda k: k % RING < 2)
    from_east = send_lon(own, 1, lambda k: k % 2 == 0)
    late = send_lon(on_chip, 0, lambda k: k % RING >= 2)
    cores, after = [], own
    for parity, received in ((0, from_west), (1, from_east)):
        near, far = call(
            for_parity(parity, edge_kernel),
            [((EDGE, CLAT), BF16), ((EDGE, CLAT), BF16)],
            [VMEM] * 5,
            [],
            1,
            1,
        )(received, own, early, late, after)
        after = near
        near = swap_lat(near, 0, parity)
        far = swap_lat(far, 1, parity)
        core = call(
            for_parity(parity, core_kernel),
            [
                ((CLON, NV, CLAT), F32),
                ((CLAT, KX), BF16),
                ((CLAT, 2 * CLAT), F32),
            ],
            [VMEM] * 6,
            [
                pltpu.VMEM((KX, 10 * CLAT), BF16),
                pltpu.VMEM((KX, CLON * CLAT), BF16),
                pltpu.VMEM((NV, 10 * CLAT), BF16),
                pltpu.VMEM((LON_REACH + 1, CLAT, CLAT), F32),
            ],
            200 << 20,
            4 << 20,
        )(level_weights.reshape(1, 2), received, own, early, late, near)
        cores.append((*core, far))
    result = ((NV * CLON, CLAT), F32)
    (even_out,) = call(for_parity(0, rim_kernel), [result], [VMEM] * 4, [], 8 << 20, 1 << 19)(*cores[0])
    (out,) = call(last_kernel, [result], [VMEM] * 5, [], 8 << 20, 1 << 19)(even_out, *cores[1])
    return out.reshape(NV, CLON, CLAT)


def solution(mesh):
    in_specs = (P(None, "lon", "lat"), P(None, "lon", "lat"), P(None, "lon", "lat"), P())
    out_specs = P(None, "lon", "lat")
    return jax.shard_map(
        per_device, mesh=mesh, in_specs=in_specs, out_specs=out_specs, check_vma=False
    )
```

```python
import jax
import jax.numpy as jnp
from jax import lax
from jax.experimental import pallas as pl
from jax.experimental.pallas import tpu as pltpu
from jax.sharding import PartitionSpec as P

KF, KC, NV = 32, 128, 32
CLON, CLAT = 4, 128
LON_REACH, LAT_REACH = 3, 16
FV = KF + NV
KX = KF + KC + KF
SENT = 3 * FV + 2 * KC
TILE = 4 * FV + 2 * KC
PADDED, EASTWARD, EARLY = 536, 472, 464
EDGE = KC + FV
COLUMNS = range(1, 11)
RING = 16
VMEM = pl.BlockSpec(memory_space=pltpu.VMEM)
F32, BF16 = jnp.float32, jnp.bfloat16

OWN_FV = (0, 64, 128, 448)
OWN_C = (192, 320)
WEST_FV = (None, 0, 64, 384)
WEST_C = (128, 256)
EAST_FV = (0, 64, 128, None)
EAST_C = (192, 320)


def lon_weight(distance):
    return 1.0 - 0.75 * (distance / LON_REACH) ** 2


class Hood:
    def __init__(self, parity, off_chip, own, early, late):
        self.parity, self.off_chip, self.own, self.early, self.late = parity, off_chip, own, early, late
        self.is_early = lax.axis_index("lon") % RING < 2

    def rows(self, tile, at, count):
        if tile == 1:
            return self.own[at : at + count, :]
        if (tile == 0) == (self.parity == 0):
            return self.off_chip[at : at + count, :]
        early, late = self.early[at : at + count, :], self.late[at : at + count, :]
        return jnp.where(self.is_early, early, late)

    def fv(self, column):
        tile, at = divmod(column, CLON)
        return self.rows(tile, (WEST_FV, OWN_FV, EAST_FV)[tile][at], FV)

    def coarse(self, column):
        tile, at = divmod(column, 2)
        return self.rows(tile, (WEST_C, OWN_C, EAST_C)[tile][at], KC)


def pack_kernel(
    fine, coarse, vectors, own, to_east, early, on_chip, fine16, coarse16, vectors16, fine32, coarse32, vectors32, sem
):
    half = KC
    pairs = (
        (fine, fine16),
        (coarse.at[:half], coarse16.at[:half]),
        (coarse.at[half:], coarse16.at[half:]),
        (vectors, vectors16),
    )
    copies = [pltpu.make_async_copy(src, dst, sem.at[n]) for n, (src, dst) in enumerate(pairs)]
    for n in (1, 2, 0, 3):
        copies[n].start()
    odd = lax.axis_index("lon") % 2 == 1

    def put(block, at):
        own[at : at + block.shape[0], :] = block

    copies[0].wait()
    fine32[...] = fine16[...].astype(F32)
    for a in range(CLON):
        put(fine32[pl.ds(a, KF, stride=CLON), :].astype(BF16), OWN_FV[a])
    copies[3].wait()
    vectors32[...] = vectors16[...].astype(F32)
    for a in range(CLON):
        put(vectors32[pl.ds(a, NV, stride=CLON), :].astype(BF16), OWN_FV[a] + KF)
    copies[1].wait()
    copies[2].wait()
    coarse32[...] = coarse16[...].astype(F32)
    for m in range(2):
        put(coarse32[pl.ds(m, KC, stride=2), :].astype(BF16), OWN_C[m])
    own[TILE:, :] = jnp.zeros((PADDED - TILE, CLAT), BF16)
    to_east[:SENT, :] = own[FV:TILE, :]
    to_east[SENT:, :] = jnp.zeros((EASTWARD - SENT, CLAT), BF16)
    trimmed = jnp.where(odd, own[:SENT, :], own[FV:TILE, :])
    early[:SENT, :] = trimmed
    early[SENT:, :] = jnp.zeros((EARLY - SENT, CLAT), BF16)
    on_chip[...] = trimmed


def for_parity(parity, body):
    def kernel(*refs):
        @pl.when(lax.axis_index("lon") % 2 == parity)
        def _():
            body(parity, *refs)

    return kernel


def edge_kernel(parity, off_chip, own, early, late, after, near, far):
    hood = Hood(parity, off_chip, own, early, late)
    odd = lax.axis_index("lat") % 2 == 1
    lane = lax.broadcasted_iota(jnp.int32, (1, CLAT), 1) // LAT_REACH

    def gather(blocks, at):
        high = jnp.zeros((FV, CLAT), BF16)
        low = jnp.zeros((FV, CLAT), BF16)
        for slot, block in blocks.items():
            shift = (slot + 1) % 8 * LAT_REACH
            moved = pltpu.roll(block, shift, 1) if shift else block
            high = jnp.where(lane == slot, moved, high)
            low = jnp.where(lane == (slot + 1) % 8, moved, low)
        near[at : at + FV, :] = jnp.where(odd, low, high)
        far[at : at + FV, :] = jnp.where(odd, high, low)

    even = {m: hood.fv(2 * m) for m in range(1, 6)}
    uneven = {m: hood.fv(2 * m + 1) for m in range(0, 5)}
    coarse = {m: hood.coarse(m) for m in range(6)}
    upper = {m: block[:FV] for m, block in coarse.items()}
    upper.update({6: even[3], 7: even[4]})
    gather(upper, 0)
    gather({m: block[FV:] for m, block in coarse.items()}, FV)
    gather({**uneven, 5: even[5], 6: even[1], 7: even[2]}, KC)


def anomaly_rows(fine, refined):
    fine = fine - jnp.mean(fine, axis=0, keepdims=True)
    coarse = refined - jnp.mean(refined, axis=0, keepdims=True)
    paired = refined[:KF]
    paired = paired - jnp.mean(paired, axis=0, keepdims=True)
    return fine, coarse, paired


def rim_taper(is_above, parity):
    above = is_above.astype(jnp.int32)
    row = lax.broadcasted_iota(jnp.int32, (CLAT, CLAT), 0)
    lane = lax.broadcasted_iota(jnp.int32, (CLAT, CLAT), 1)
    column = 2 * (lane // LAT_REACH - above) + parity
    lon_gap = jnp.abs(column - CLON - row // (2 * LAT_REACH))
    shift = lane % LAT_REACH - row % LAT_REACH
    lat_gap = LAT_REACH + (2 * above - 1) * shift
    lon_ratio = lon_gap.astype(F32) * (1.0 / LON_REACH)
    lat_ratio = lat_gap.astype(F32) * (1.0 / LAT_REACH)
    here = row // LAT_REACH % 2 + above == 1
    inside = here & (lon_gap <= LON_REACH) & (lat_gap <= LAT_REACH)
    value = (1.0 - 0.75 * lon_ratio * lon_ratio) * (1.0 - 0.75 * lat_ratio * lat_ratio)
    return jnp.where(inside, value, 0.0)


def halfway(values):
    return 0.5 * (values + pltpu.roll(values, CLAT - LAT_REACH, 1))


def rim_terms(rim, edges, taper, is_above):
    refined = rim[:KC].astype(F32)
    coarse = refined - jnp.mean(refined, axis=0, keepdims=True)
    paired = refined[:KF] - jnp.mean(refined[:KF], axis=0, keepdims=True)
    slot = lax.broadcasted_iota(jnp.int32, (1, CLAT), 1) // LAT_REACH
    own_slot = (slot + 8 - is_above.astype(jnp.int32)) % 8
    mixed = rim[KC:].astype(F32)
    even = jnp.where(own_slot <= 2, pltpu.roll(mixed, 3 * LAT_REACH, 1), pltpu.roll(refined[:FV], 5 * LAT_REACH, 1))
    even = jnp.where(own_slot >= 5, mixed, even)
    hood, vectors = [], []
    for values, pair in ((even, (coarse, paired)), (mixed, (halfway(coarse), halfway(paired)))):
        fine = values[:KF] - jnp.mean(values[:KF], axis=0, keepdims=True)
        hood.append(jnp.concatenate([part.astype(BF16) for part in (fine, *pair)], axis=0))
        vectors.append(values[KF:].astype(BF16))
    gram = jnp.dot(edges, jnp.concatenate(hood, axis=1), preferred_element_type=F32)
    added = lax.dot_general(
        jnp.concatenate(vectors, axis=1),
        (taper * gram).astype(BF16),
        (((1,), (1,)), ((), ())),
        preferred_element_type=F32,
    )
    outer = (slot == 0) | (slot == 7)
    return [
        jnp.where(outer, pltpu.roll(added, (7 - 2 * a) * LAT_REACH, 1), 0.0) for a in range(CLON)
    ]


def core_kernel(
    parity, weights, off_chip, own, early, late, near, out, edges, far_taper, hood, mine, vectors, taper
):
    tiles = Hood(parity, off_chip, own, early, late)
    i = lax.broadcasted_iota(jnp.int32, (CLAT, CLAT), 0)
    j = lax.broadcasted_iota(jnp.int32, (CLAT, CLAT), 1)
    gap = jnp.abs(i - j)
    ratio = gap.astype(F32) * (1.0 / LAT_REACH)
    band = jnp.where(gap <= LAT_REACH, 1.0 - 0.75 * ratio * ratio, 0.0)
    for distance in range(LON_REACH + 1):
        taper[distance] = band * lon_weight(distance)
    level = weights[...]
    weight_fine = level[:, :1] * (1.0 / (KF - 1))
    weight_coarse = level[:, 1:] * (1.0 / (KC - 1))
    weight_paired = level[:, 1:] * (-1.0 / (KF - 1))
    lane = lax.broadcasted_iota(jnp.int32, (1, CLAT), 1) // LAT_REACH
    both = jnp.zeros((KX, CLAT), F32)
    coarse_columns = [tiles.coarse(m).astype(F32) for m in range(6)]
    for b in COLUMNS:
        block = tiles.fv(b)
        refined = coarse_columns[b // 2]
        if b % 2:
            refined = 0.5 * (refined + coarse_columns[b // 2 + 1])
        fine, coarse, paired = anomaly_rows(block[:KF].astype(F32), refined)
        lanes = slice((b - 1) * CLAT, b * CLAT)
        hood[:KF, lanes] = fine.astype(BF16)
        hood[KF : KF + KC, lanes] = coarse.astype(BF16)
        hood[KF + KC :, lanes] = paired.astype(BF16)
        vectors[:, lanes] = block[KF:]
        if CLON <= b < 2 * CLON:
            a = b - CLON
            scaled = jnp.concatenate(
                (weight_fine * fine, weight_coarse * coarse, weight_paired * paired), axis=0
            )
            mine[:, a * CLAT : (a + 1) * CLAT] = scaled.astype(BF16)
            moved = pltpu.roll(scaled, (2 * a + 1) * LAT_REACH, 1)
            both = jnp.where(lane // 2 == a, moved, both)
    edges[...] = both.T.astype(BF16)
    odd = lax.axis_index("lat") % 2 == 1
    far_taper[...] = jnp.concatenate([rim_taper(odd, n) for n in range(2)], axis=1)
    near_taper = jnp.concatenate([rim_taper(~odd, n) for n in range(2)], axis=1)
    near_terms = rim_terms(near[...], edges[...], near_taper, ~odd)
    for a in range(CLON):
        lanes = slice(a * CLAT, (a + 7) * CLAT)
        gram = lax.dot_general(
            mine[:, a * CLAT : (a + 1) * CLAT],
            hood[:, lanes],
            (((0,), (0,)), ((), ())),
            preferred_element_type=F32,
        )
        tapered = jnp.concatenate(
            [
                (taper[abs(n - LON_REACH)] * gram[:, n * CLAT : (n + 1) * CLAT]).astype(BF16)
                for n in range(7)
            ],
            axis=1,
        )
        out[a] = near_terms[a] + lax.dot_general(
            vectors[:, lanes], tapered, (((1,), (1,)), ((), ())), preferred_element_type=F32
        )


def rim_kernel(parity, core, edges, far_taper, far, out):
    odd = lax.axis_index("lat") % 2 == 1
    terms = rim_terms(far[...], edges[...], far_taper[...], odd)
    for a in range(CLON):
        out[pl.ds(a, NV, stride=CLON), :] = core[a] + terms[a]


def last_kernel(even_out, core, edges, far_taper, far, out):
    odd = lax.axis_index("lon") % 2 == 1

    @pl.when(odd)
    def _():
        rim_kernel(1, core, edges, far_taper, far, out)

    @pl.when(~odd)
    def _():
        out[...] = even_out[...]


def call(kernel, outs, in_specs, scratch, flops, moved):
    return pl.pallas_call(
        kernel,
        out_shape=[jax.ShapeDtypeStruct(shape, dtype) for shape, dtype in outs],
        in_specs=in_specs,
        out_specs=[VMEM] * len(outs),
        scratch_shapes=scratch,
        compiler_params=pltpu.CompilerParams(vmem_limit_bytes=24 << 20),
        cost_estimate=pl.CostEstimate(flops=flops, bytes_accessed=moved, transcendentals=0),
    )


def in_hbm(array):
    return pltpu.with_memory_space_constraint(array, pltpu.HBM)


def partner(k, first):
    return ((k - first) ^ 1) + first


def swap_lat(block, first, parity):
    lon, lat = lax.axis_size("lon"), lax.axis_size("lat")
    pairs = [(k, partner(k, first)) for k in range(lat) if 0 <= partner(k, first) < lat]
    pairs = [(n * lat + k, n * lat + to) for n in range(parity, lon, 2) for k, to in pairs]
    return lax.ppermute(block, ("lon", "lat"), pairs)


def send_lon(block, first, chosen):
    n = lax.axis_size("lon")
    return lax.ppermute(block, "lon", [(k, partner(k, first) % n) for k in range(n) if chosen(k)])


def per_device(fine_members, coarse_members, increments, level_weights):
    shapes = ((128, CLAT), (256, CLAT), (128, CLAT))
    own, to_east, early, on_chip = call(
        pack_kernel,
        [((rows, CLAT), BF16) for rows in (PADDED, EASTWARD, EARLY, SENT)],
        [pl.BlockSpec(memory_space=pltpu.HBM)] * 3,
        [pltpu.VMEM(shape, BF16) for shape in shapes]
        + [pltpu.VMEM(shape, F32) for shape in shapes]
        + [pltpu.SemaphoreType.DMA((4,))],
        1 << 20,
        1 << 19,
    )(
        in_hbm(fine_members.reshape(KF * CLON, CLAT)),
        in_hbm(coarse_members.reshape(KC * 2, CLAT)),
        in_hbm(increments.reshape(NV * CLON, CLAT)),
    )
    from_west = send_lon(to_east, 1, lambda k: k % 2 == 1)
    early = send_lon(early, 0, lambda k: k % RING < 2)
    from_east = send_lon(own, 1, lambda k: k % 2 == 0)
    late = send_lon(on_chip, 0, lambda k: k % RING >= 2)
    cores, after = [], own
    for parity, received in ((0, from_west), (1, from_east)):
        near, far = call(
            for_parity(parity, edge_kernel),
            [((EDGE, CLAT), BF16), ((EDGE, CLAT), BF16)],
            [VMEM] * 5,
            [],
            1,
            1,
        )(received, own, early, late, after)
        after = near
        near = swap_lat(near, 0, parity)
        far = swap_lat(far, 1, parity)
        core = call(
            for_parity(parity, core_kernel),
            [
                ((CLON, NV, CLAT), F32),
                ((CLAT, KX), BF16),
                ((CLAT, 2 * CLAT), F32),
            ],
            [VMEM] * 6,
            [
                pltpu.VMEM((KX, 10 * CLAT), BF16),
                pltpu.VMEM((KX, CLON * CLAT), BF16),
                pltpu.VMEM((NV, 10 * CLAT), BF16),
                pltpu.VMEM((LON_REACH + 1, CLAT, CLAT), F32),
            ],
            200 << 20,
            4 << 20,
        )(level_weights.reshape(1, 2), received, own, early, late, near)
        cores.append((*core, far))
    result = ((NV * CLON, CLAT), F32)
    (even_out,) = call(for_parity(0, rim_kernel), [result], [VMEM] * 4, [], 8 << 20, 1 << 19)(*cores[0])
    (out,) = call(last_kernel, [result], [VMEM] * 5, [], 8 << 20, 1 << 19)(even_out, *cores[1])
    return out.reshape(NV, CLON, CLAT)


def solution(mesh):
    in_specs = (P(None, "lon", "lat"), P(None, "lon", "lat"), P(None, "lon", "lat"), P())
    out_specs = P(None, "lon", "lat")
    return jax.shard_map(
        per_device, mesh=mesh, in_specs=in_specs, out_specs=out_specs, check_vma=False
    )
```
